1024 devices in a mesh: seq: 64 (over z_hi, y, x), head: 16 (over z_lo, core).
Axes of the slice: x: 4, y: 8, z: 16 (z_hi: 2, z_lo: 8; z = z_hi * 8 + z_lo), core: 2. Of those that a mesh axis runs over, the one named last changes fastest.
Arguments:
- queries: bfloat16 [8192, 2048], P('seq', 'head'), may hold values from -108 to 108
- key_rows: bfloat16 [8192, 2048], P('seq', 'head'), may hold values from -4.5 to 4.5
- value_rows: bfloat16 [8192, 2048], P('seq', 'head'), may hold values from -6 to 6
- out_weight: bfloat16 [2048, 2048], P('head'), may hold values from -4 to 4
- strided_index: int32 [64, 8], P('seq'), may hold values from 0 to 15
- cotangent: bfloat16 [8192, 2048], P('seq'), may hold values from -6 to 6
Outputs:
- mixed_output: bfloat16 [8192, 2048], P('seq', 'head')
- grad_queries: bfloat16 [8192, 2048], P('seq', 'head')
- grad_keys: bfloat16 [8192, 2048], P('seq', 'head')
- grad_values: bfloat16 [8192, 2048], P('seq', 'head')
The draws below stay inside these ranges and needn't reach their ends.
All inputs are finite; a program needn't handle non-finite values.
Results may differ from the reference program's by a relative error of at most 0.023.
Values may be sent and summed in bfloat16 or wider, within the bound.
A program may use at most 32 MiB of HBM per device.

```python
import jax
import jax.numpy as jnp
from jax import lax

HD = 128
D = 2048
BLK = 128
NSTR = 8
STRIDE_ROWS = 32
TOK_DEV = 128
HEADS = 16
TOKENS = 8192
NBLK = 64
NSB = 16


def draw_pair(key):
    base = jax.random.fold_in(key, 7)
    first, second = jax.random.split(base, 2)
    shaped = (TOKENS, HEADS * HD)
    key_values = jnp.clip(jax.random.normal(first, shaped, jnp.float32), -4.5, 4.5)
    query_values = jnp.clip(jax.random.normal(second, shaped, jnp.float32), -4.5, 4.5)
    return (query_values, key_values)


def draw_queries(key, part):
    return draw_pair(key)[0].astype(jnp.bfloat16)


def draw_key_rows(key, part):
    return draw_pair(key)[1].astype(jnp.bfloat16)


def place_ends(result, own_key, smallest, high):
    spot = [jax.random.randint(jax.random.fold_in(own_key, axis), (), 0, length) for axis, length in enumerate(result.shape)]
    longest = result.shape.index(max(result.shape))
    beside = spot[:longest] + [(spot[longest] + 1) % result.shape[longest]] + spot[longest + 1:]
    return result.at[tuple(spot)].set(smallest).at[tuple(beside)].set(high)


def level_of(rng, dims, cuts, low, largest):
    def one(dim, shards_of):
        draws = jax.random.uniform(jax.random.fold_in(jax.random.fold_in(rng, 6), dim), (shards_of,), jnp.float32, low / len(cuts), largest / len(cuts))
        return jnp.repeat(jnp.exp(draws), dims[dim] // shards_of).reshape((-1,) + (1,) * (len(dims) - dim - 1))

    loudness = one(*cuts[0])
    for cut in cuts[1:]:
        loudness = loudness * one(*cut)
    return loudness


def scatter_about(stream_key, shape, spread, most, cuts=(), kind=jnp.bfloat16):
    result = spread * jax.random.normal(stream_key, shape, jnp.float32)
    if cuts:
        result = result * level_of(stream_key, shape, cuts, -0.22, 0.18)
    return jnp.clip(result, -most, most).astype(kind)


def setup_inputs(seed: int = 0) -> dict:
    streams_of = jax.random.split(jax.random.key(seed), 7)
    return {
        "queries": draw_queries(jax.random.fold_in(streams_of[6], 71), 0),
        "key_rows": draw_key_rows(jax.random.fold_in(streams_of[6], 71), 0),
        "value_rows": scatter_about(streams_of[2], (TOKENS, HEADS * HD), 1.0, 6.0, ((0, 64), (1, 16))),
        "out_weight": scatter_about(streams_of[3], (HEADS * HD, D), 2 ** -0.5, 4.0, ((0, 16),)),
        "strided_index": place_ends(jax.random.randint(streams_of[4], (NBLK, NSTR), 0, NSB), jax.random.fold_in(streams_of[4], 1), 0, NSB - 1).astype(jnp.int32),
        "cotangent": scatter_about(streams_of[5], (TOKENS, D), 1.0, 6.0, ((0, 64),)),
    }


def strided_tokens():
    number = jnp.arange(NSB * BLK, dtype=jnp.int32)
    return (number // STRIDE_ROWS) * TOK_DEV + number % STRIDE_ROWS


def block_list(blocks, strided_blocks, index_row, position):
    count = blocks.shape[0]
    window = jnp.stack([blocks[(position - 1) % count], blocks[position], blocks[(position + 1) % count]])
    picked = strided_blocks[index_row]
    joined = jnp.concatenate([window, picked], axis=0)
    return joined.reshape(-1, blocks.shape[2], blocks.shape[3])


def probability_of(query_block, key_list):
    scores = jnp.einsum('qhd,khd->hqk', query_block.astype(jnp.float32), key_list.astype(jnp.float32)) * (HD ** -0.5)
    row_top = jnp.max(scores, axis=-1, keepdims=True)
    logsum = row_top + jnp.log(jnp.sum(jnp.exp(scores - row_top), axis=-1, keepdims=True))
    return jnp.exp(scores - logsum)


def reference(queries, key_rows, value_rows, out_weight, strided_index, cotangent):
    tokens = queries.shape[0]
    count = tokens // BLK
    shaped = (count, BLK, HEADS, HD)
    query_blocks = queries.reshape(shaped)
    key_blocks = key_rows.reshape(shaped)
    value_blocks = value_rows.reshape(shaped)
    chosen = strided_tokens()
    key_strided = key_rows.reshape(tokens, HEADS, HD)[chosen].reshape(NSB, BLK, HEADS, HD)
    value_strided = value_rows.reshape(tokens, HEADS, HD)[chosen].reshape(NSB, BLK, HEADS, HD)
    numbers = jnp.arange(count, dtype=jnp.int32)

    def forward(position):
        key_list = block_list(key_blocks, key_strided, strided_index[position], position)
        value_list = block_list(value_blocks, value_strided, strided_index[position], position)
        weights = probability_of(query_blocks[position], key_list).astype(jnp.bfloat16)
        output = jnp.einsum('hqk,khd->qhd', weights.astype(jnp.float32), value_list.astype(jnp.float32))
        return output.astype(jnp.bfloat16)

    attention = lax.map(forward, numbers).reshape(tokens, HEADS * HD)
    mixed_output = jnp.dot(attention, out_weight, preferred_element_type=jnp.float32).astype(jnp.bfloat16)
    grad_attention = jnp.dot(cotangent, out_weight.T, preferred_element_type=jnp.float32).astype(jnp.bfloat16)
    grad_blocks = grad_attention.reshape(shaped)

    def backward(state_pair, position):
        key_sum, value_sum, key_side, value_side = state_pair
        key_list = block_list(key_blocks, key_strided, strided_index[position], position)
        value_list = block_list(value_blocks, value_strided, strided_index[position], position)
        query_block = query_blocks[position].astype(jnp.float32)
        grad_block = grad_blocks[position].astype(jnp.float32)
        probability = probability_of(query_blocks[position], key_list)
        weights = probability.astype(jnp.bfloat16)
        grad_weights = jnp.einsum('qhd,khd->hqk', grad_block, value_list.astype(jnp.float32))
        row_delta = jnp.sum(probability * grad_weights, axis=-1, keepdims=True)
        grad_scores = (probability * (grad_weights - row_delta) * (HD ** -0.5)).astype(jnp.bfloat16)
        grad_query = jnp.einsum('hqk,khd->qhd', grad_scores.astype(jnp.float32), key_list.astype(jnp.float32)).astype(jnp.bfloat16)
        key_terms = jnp.einsum('hqk,qhd->khd', grad_scores.astype(jnp.float32), query_block)
        value_terms = jnp.einsum('hqk,qhd->khd', weights.astype(jnp.float32), grad_block)
        places = jnp.stack([(position - 1) % count, position, (position + 1) % count]).astype(jnp.int32)
        key_sum = key_sum.at[places].add(key_terms[:3 * BLK].reshape(3, BLK, HEADS, HD))
        value_sum = value_sum.at[places].add(value_terms[:3 * BLK].reshape(3, BLK, HEADS, HD))
        picks = strided_index[position]
        key_side = key_side.at[picks].add(key_terms[3 * BLK:].reshape(-1, BLK, HEADS, HD))
        value_side = value_side.at[picks].add(value_terms[3 * BLK:].reshape(-1, BLK, HEADS, HD))
        return (key_sum, value_sum, key_side, value_side), grad_query

    start_state = (jnp.zeros(shaped, jnp.float32), jnp.zeros(shaped, jnp.float32),
                   jnp.zeros((NSB, BLK, HEADS, HD), jnp.float32), jnp.zeros((NSB, BLK, HEADS, HD), jnp.float32))
    final_state, grad_parts = lax.scan(backward, start_state, numbers)
    key_sum, value_sum, key_side, value_side = final_state
    key_total = key_sum.reshape(tokens, HEADS, HD).at[chosen].add(key_side.reshape(NSB * BLK, HEADS, HD))
    value_total = value_sum.reshape(tokens, HEADS, HD).at[chosen].add(value_side.reshape(NSB * BLK, HEADS, HD))
    grad_queries = grad_parts.reshape(tokens, HEADS * HD)
    grad_keys = key_total.reshape(tokens, HEADS * HD).astype(jnp.bfloat16)
    grad_values = value_total.reshape(tokens, HEADS * HD).astype(jnp.bfloat16)
    return (mixed_output, grad_queries, grad_keys, grad_values)
```

```python
import functools

import jax
import jax.numpy as jnp
from jax import lax
from jax.experimental import pallas as pl
from jax.experimental.pallas import tpu as pltpu
from jax.sharding import PartitionSpec as P

HD = 128
BLK = 128
ROWS = 32
GRID = (2, 8, 4)
GROUP = 4
MESH = pl.DeviceIdType.MESH
F32 = jnp.float32
BF16 = jnp.bfloat16
SCALE = HD ** -0.5
EXCLUDED = -1e30


def nt(a, b):
    return lax.dot_general(a, b, (((1,), (1,)), ((), ())), preferred_element_type=F32)


def nn(a, b):
    return lax.dot_general(a, b, (((1,), (0,)), ((), ())), preferred_element_type=F32)


def tn(a, b):
    return lax.dot_general(a, b, (((0,), (0,)), ((), ())), preferred_element_type=F32)


def kernel(
    dims, group, heads,
    q_hbm, k_hbm, v_hbm, w_hbm, index_ref, ct_hbm,
    mixed_ref, gq_ref, gk_ref, gv_ref,
    w_ref, ct_ref, win, kvg, qdo, bias, wg, stats, osend, orecv, attg, msend, mrecv,
    dqs, dqr, gws, gwr, gs, gy, gzs, gzr, s_ref, dw_ref,
    local_sem, w_local_sem,
    z_s, z_r, y_s, y_r, win_s, win_r, qdo_s, qdo_r, bias_s, bias_r, w_s, w_r,
    st_s, st_r, o_s, o_r, dq_s, dq_r, gw_s, gw_r, gy_s, gy_r, gz_s, gz_r, att_s, att_r, mix_s, mix_r,
):
    nz, ny, nx = dims
    count = nz * ny * nx
    groups = heads // group
    seq = lax.axis_index("seq")
    head = lax.axis_index("head")
    z, y, x = seq // (ny * nx), (seq // nx) % ny, seq % nx
    g, r = head // group, head % group

    def at(dz, dy, dx):
        return (((z + dz) % nz * ny + (y + dy) % ny) * nx + (x + dx) % nx, head)

    def member(d):
        return (seq, g * group + (r + d) % group)

    def other_group(e):
        return (seq, (g + e) % groups * group + r)

    following = ((seq + 1) % count, head)
    preceding = ((seq + count - 1) % count, head)

    def send(src, dst, send_sem, recv_sem, device):
        return pltpu.make_async_remote_copy(
            src_ref=src, dst_ref=dst, send_sem=send_sem, recv_sem=recv_sem,
            device_id=device, device_id_type=MESH,
        )

    started = []

    def start(src, dst, send_sem, recv_sem, device):
        copy = send(src, dst, send_sem, recv_sem, device)
        copy.start()
        started.append(copy)

    def received(dst, send_sem, recv_sem):
        send(dst, dst, send_sem, recv_sem, at(1, 0, 0)).wait_recv()

    loads = [
        pltpu.make_async_copy(k_hbm, win.at[1, 0], local_sem.at[0]),
        pltpu.make_async_copy(v_hbm, win.at[1, 1], local_sem.at[1]),
        pltpu.make_async_copy(q_hbm, qdo.at[0, 0], local_sem.at[2]),
        pltpu.make_async_copy(w_hbm, w_ref, local_sem.at[3]),
        pltpu.make_async_copy(ct_hbm, ct_ref, local_sem.at[4]),
    ]
    for load in loads:
        load.start()

    partners = [at(1, 0, 0)]
    partners += [at(0, d, 0) for d in range(1, ny)]
    partners += [at(0, 0, d) for d in range(1, nx)]
    partners += [following, preceding]
    partners += [member(d) for d in range(1, group)]
    partners += [other_group(e) for e in range(1, groups)]
    barrier = pltpu.get_barrier_semaphore()
    for device in partners:
        pl.semaphore_signal(barrier, inc=1, device_id=device, device_id_type=MESH)

    row = lax.broadcasted_iota(jnp.int32, (nz * ny, BLK), 0)
    block = ((z + row // ny) % nz * ny + (y + row % ny) % ny) * nx // (BLK // ROWS)
    listed = jnp.zeros((nz * ny, BLK), F32)
    for slot in range(index_ref.shape[1]):
        listed = listed + (block == index_ref[0, slot]).astype(F32)
    bias[0] = jnp.where(listed > 0, jnp.log(jnp.maximum(listed, 1.0)), EXCLUDED)

    loads[0].wait()
    loads[1].wait()
    kvg[0, 0] = win[1, :, :ROWS, :]
    pl.semaphore_wait(barrier, len(partners))

    start(kvg.at[0, 0], kvg.at[1, 0], z_s.at[0], z_r.at[0], at(1, 0, 0))
    for d in range(1, ny):
        start(kvg.at[0, 0], kvg.at[0, ny - d], y_s.at[0, d], y_r.at[0, d], at(0, d, 0))
    start(win.at[1], win.at[0], win_s.at[0], win_r.at[0], following)
    start(win.at[1], win.at[2], win_s.at[1], win_r.at[1], preceding)
    for d in range(1, nx):
        start(bias.at[0], bias.at[nx - d], bias_s.at[d], bias_r.at[d], at(0, 0, d))

    loads[2].wait()
    loads[3].wait()
    loads[4].wait()
    qdo[0, 1] = nt(ct_ref[...], w_ref[...]).astype(BF16)
    for d in range(1, nx):
        start(qdo.at[0], qdo.at[nx - d], qdo_s.at[d], qdo_r.at[d], at(0, 0, d))

    received(kvg.at[1, 0], z_s.at[0], z_r.at[0])
    for d in range(1, ny):
        start(kvg.at[1, 0], kvg.at[1, ny - d], y_s.at[1, d], y_r.at[1, d], at(0, d, 0))

    def columns(e, d):
        return pl.ds(pl.multiple_of(((g + e) % groups * group + (r + d) % group) * HD, HD), HD)

    w_loads = []
    for e in range(groups):
        to = pl.ds(e * HD, HD)
        load = pltpu.make_async_copy(w_hbm.at[:, columns(e, 0)], wg.at[0, :, to], w_local_sem.at[e])
        load.start()
        w_loads.append(load)
        for d in range(1, group):
            start(w_hbm.at[:, columns(e, d)], wg.at[group - d, :, to], w_s.at[d, e], w_r.at[d, e], member(d))

    received(win.at[0], win_s.at[0], win_r.at[0])
    received(win.at[2], win_s.at[1], win_r.at[1])
    key_w = win[:, 0].reshape(3 * BLK, HD)
    value_w = win[:, 1].reshape(3 * BLK, HD)
    query_own, grad_own = qdo[0, 0], qdo[0, 1]
    score_w = nt(key_w, query_own) * SCALE
    top_w = jnp.max(score_w, axis=0, keepdims=True)
    p_w = jnp.exp(score_w - top_w)
    sum_w = jnp.sum(p_w, axis=0, keepdims=True)
    dw_w = nt(value_w, grad_own)
    delta_w = jnp.sum(p_w * dw_w, axis=0, keepdims=True)
    o_w = tn(value_w, p_w.astype(BF16))

    for d in range(1, nx):
        received(bias.at[nx - d], bias_s.at[d], bias_r.at[d])
        received(qdo.at[nx - d], qdo_s.at[d], qdo_r.at[d])
    for plane in range(2):
        for d in range(1, ny):
            received(kvg.at[plane, ny - d], y_s.at[plane, d], y_r.at[plane, d])
    chunks = nz * ny
    keys = kvg[:, :, 0].reshape(chunks * ROWS, HD)
    values = kvg[:, :, 1].reshape(chunks * ROWS, HD)
    queries = qdo[:, 0].reshape(nx * BLK, HD)
    grads = qdo[:, 1].reshape(nx * BLK, HD)
    s_ref[...] = nt(keys, queries)
    dw_ref[...] = nt(values, grads)
    tops, sums, deltas = [], [], []
    for i in range(nx):
        lanes = pl.ds(i * BLK, BLK)
        spread = jnp.broadcast_to(bias[i][:, None, :], (chunks, ROWS, BLK)).reshape(chunks * ROWS, BLK)
        score = s_ref[:, lanes] * SCALE + spread
        top = jnp.max(score, axis=0, keepdims=True)
        p = jnp.exp(score - top)
        s_ref[:, lanes] = p
        tops.append(top)
        sums.append(jnp.sum(p, axis=0, keepdims=True))
        deltas.append(jnp.sum(p * dw_ref[:, lanes], axis=0, keepdims=True))
    for i in range(nx):
        top, total, delta = tops[i], sums[i], deltas[i]
        if i == 0:
            top = jnp.maximum(tops[0], top_w)
            a, b = jnp.exp(tops[0] - top), jnp.exp(top_w - top)
            total = a * sums[0] + b * sum_w
            delta = a * deltas[0] + b * delta_w
        stats[0, i, 0:1, :] = top
        stats[0, i, 1:2, :] = total
        stats[0, i, 2:3, :] = delta
        stats[0, i, 3:8, :] = jnp.zeros((5, BLK), F32)
    for d in range(1, nx):
        start(stats.at[0], stats.at[nx - d], st_s.at[d], st_r.at[d], at(0, 0, d))
    o_part = tn(values, s_ref[...].astype(BF16))
    for d in range(1, nx):
        osend[d] = o_part[:, d * BLK:(d + 1) * BLK].astype(BF16)
        start(osend.at[d], orecv.at[nx - d], o_s.at[d], o_r.at[d], at(0, 0, d))
    for d in range(1, nx):
        received(stats.at[nx - d], st_s.at[d], st_r.at[d])

    logsums, all_deltas = [], []
    for i in range(nx):
        entries = [(stats[p, (i - p) % nx, 0:1, :], stats[p, (i - p) % nx, 1:2, :], stats[p, (i - p) % nx, 2:3, :]) for p in range(nx)]
        top = functools.reduce(jnp.maximum, [e[0] for e in entries])
        logsum = top + jnp.log(sum(e[1] * jnp.exp(e[0] - top) for e in entries))
        logsums.append(logsum)
        all_deltas.append(sum(e[2] * jnp.exp(e[0] - logsum) for e in entries))

    factor_w = jnp.exp(top_w - logsums[0])
    attention = o_part[:, :BLK] * jnp.exp(tops[0] - logsums[0]) + o_w * factor_w
    for d in range(1, nx):
        p = nx - d
        received(orecv.at[p], o_s.at[d], o_r.at[d])
        attention = attention + orecv[p].astype(F32) * jnp.exp(stats[p, (-p) % nx, 0:1, :] - logsums[0])
    attg[0] = attention.astype(BF16)
    for d in range(1, group):
        start(attg.at[0], attg.at[group - d], att_s.at[d], att_r.at[d], member(d))

    weights, grad_scores = [], []
    for i in range(nx):
        lanes = pl.ds(i * BLK, BLK)
        probability = s_ref[:, lanes] * jnp.exp(tops[i] - logsums[i])
        weights.append(probability.astype(BF16))
        grad_scores.append((probability * (dw_ref[:, lanes] - all_deltas[i]) * SCALE).astype(BF16))
    weights = jnp.concatenate(weights, axis=1)
    grad_scores = jnp.concatenate(grad_scores, axis=1)
    gs[:, :, 0] = nn(grad_scores, queries).astype(BF16).reshape(nz, ny, ROWS, HD)
    gs[:, :, 1] = nn(weights, grads).astype(BF16).reshape(nz, ny, ROWS, HD)
    for plane in (1, 0):
        for d in range(1, ny):
            start(gs.at[plane, d], gy.at[plane, ny - d], gy_s.at[plane, d], gy_r.at[plane, d], at(0, d, 0))

    prob_w = p_w * factor_w
    ds_w = (prob_w * (dw_w - all_deltas[0]) * SCALE).astype(BF16)
    gk_w = nn(ds_w, query_own)
    gv_w = nn(prob_w.astype(BF16), grad_own)
    gws[0, 0] = gk_w[:BLK].astype(BF16)
    gws[0, 1] = gv_w[:BLK].astype(BF16)
    gws[1, 0] = gk_w[2 * BLK:].astype(BF16)
    gws[1, 1] = gv_w[2 * BLK:].astype(BF16)
    start(gws.at[0], gwr.at[0], gw_s.at[0], gw_r.at[0], preceding)
    start(gws.at[1], gwr.at[1], gw_s.at[1], gw_r.at[1], following)

    dq = tn(keys, grad_scores)
    for d in range(1, nx):
        dqs[d] = dq[:, d * BLK:(d + 1) * BLK].astype(BF16)
        start(dqs.at[d], dqr.at[nx - d], dq_s.at[d], dq_r.at[d], at(0, 0, d))
    dq_own = dq[:, :BLK] + tn(key_w, ds_w)

    for load in w_loads:
        load.wait()
    for d in range(1, group):
        for e in range(groups):
            received(wg.at[group - d, :, pl.ds(e * HD, HD)], w_s.at[d, e], w_r.at[d, e])
        received(attg.at[group - d], att_s.at[d], att_r.at[d])
    mixed = tn(attg[...].reshape(group * HD, BLK), wg[...].reshape(group * HD, groups * HD))
    for e in range(1, groups):
        msend[e] = mixed[:, e * HD:(e + 1) * HD].astype(BF16)
        start(msend.at[e], mrecv.at[groups - e], mix_s.at[e], mix_r.at[e], other_group(e))
    mixed_own = mixed[:, :HD]

    total = gs[1, 0].astype(F32)
    for d in range(1, ny):
        received(gy.at[1, ny - d], gy_s.at[1, d], gy_r.at[1, d])
        total = total + gy[1, ny - d].astype(F32)
    gzs[...] = total.astype(BF16)
    start(gzs, gzr, gz_s.at[0], gz_r.at[0], at(1, 0, 0))

    for d in range(1, nx):
        received(dqr.at[nx - d], dq_s.at[d], dq_r.at[d])
        dq_own = dq_own + dqr[nx - d].astype(F32)
    gq_ref[...] = dq_own.T.astype(BF16)

    received(gwr.at[0], gw_s.at[0], gw_r.at[0])
    received(gwr.at[1], gw_s.at[1], gw_r.at[1])
    own_k = gk_w[BLK:2 * BLK] + gwr[0, 0].astype(F32) + gwr[1, 0].astype(F32)
    own_v = gv_w[BLK:2 * BLK] + gwr[0, 1].astype(F32) + gwr[1, 1].astype(F32)
    gk_ref[ROWS:, :] = own_k[ROWS:].astype(BF16)
    gv_ref[ROWS:, :] = own_v[ROWS:].astype(BF16)

    total = gs[0, 0].astype(F32)
    for d in range(1, ny):
        received(gy.at[0, ny - d], gy_s.at[0, d], gy_r.at[0, d])
        total = total + gy[0, ny - d].astype(F32)

    for e in range(1, groups):
        received(mrecv.at[groups - e], mix_s.at[e], mix_r.at[e])
        mixed_own = mixed_own + mrecv[groups - e].astype(F32)
    mixed_ref[...] = mixed_own.astype(BF16)

    received(gzr, gz_s.at[0], gz_r.at[0])
    total = total + gzr[...].astype(F32)
    gk_ref[:ROWS, :] = (own_k[:ROWS] + total[0]).astype(BF16)
    gv_ref[:ROWS, :] = (own_v[:ROWS] + total[1]).astype(BF16)

    for copy in started:
        copy.wait_send()


def build(mesh, dims, group):
    nz, ny, nx = dims
    heads = mesh.shape["head"]
    groups = heads // group
    chunks = nz * ny

    def shards(queries, key_rows, value_rows, out_weight, strided_index, cotangent):
        width = out_weight.shape[1]
        dma = pltpu.SemaphoreType.DMA
        block = jax.ShapeDtypeStruct((BLK, HD), BF16)
        hbm = pl.BlockSpec(memory_space=pl.ANY)
        vmem = pl.BlockSpec(memory_space=pltpu.VMEM)
        square = lambda n: pltpu.VMEM((n, BLK, HD), BF16)
        pieces = lambda: pltpu.VMEM((nz, ny, 2, ROWS, HD), BF16)
        return pl.pallas_call(
            functools.partial(kernel, dims, group, heads),
            out_shape=(block,) * 4,
            in_specs=[hbm, hbm, hbm, hbm, pl.BlockSpec(memory_space=pltpu.SMEM), hbm],
            out_specs=(vmem,) * 4,
            scratch_shapes=[
                pltpu.VMEM((HD, width), BF16),
                pltpu.VMEM((BLK, width), BF16),
                pltpu.VMEM((3, 2, BLK, HD), BF16),
                pieces(),
                pltpu.VMEM((nx, 2, BLK, HD), BF16),
                pltpu.VMEM((nx, chunks, BLK), F32),
                pltpu.VMEM((group, HD, groups * HD), BF16),
                pltpu.VMEM((nx, nx, 8, BLK), F32),
                square(nx), square(nx),
                square(group),
                square(groups), square(groups),
                square(nx), square(nx),
                pltpu.VMEM((2, 2, BLK, HD), BF16), pltpu.VMEM((2, 2, BLK, HD), BF16),
                pieces(), pieces(),
                pltpu.VMEM((2, ROWS, HD), BF16), pltpu.VMEM((2, ROWS, HD), BF16),
                pltpu.VMEM((chunks * ROWS, nx * BLK), F32),
                pltpu.VMEM((chunks * ROWS, nx * BLK), F32),
                dma((5,)), dma((groups,)),
                dma((1,)), dma((1,)),
                dma((2, ny)), dma((2, ny)),
                dma((2,)), dma((2,)),
                dma((nx,)), dma((nx,)),
                dma((nx,)), dma((nx,)),
                dma((group, groups)), dma((group, groups)),
                dma((nx,)), dma((nx,)),
                dma((nx,)), dma((nx,)),
                dma((nx,)), dma((nx,)),
                dma((2,)), dma((2,)),
                dma((2, ny)), dma((2, ny)),
                dma((1,)), dma((1,)),
                dma((group,)), dma((group,)),
                dma((groups,)), dma((groups,)),
            ],
            compiler_params=pltpu.CompilerParams(
                collective_id=0, has_side_effects=True, vmem_limit_bytes=40 * 2 ** 20
            ),
        )(queries, key_rows, value_rows, out_weight, strided_index, cotangent)

    spread = P("seq", "head")
    return jax.shard_map(
        shards,
        mesh=mesh,
        in_specs=(spread, spread, spread, P("head", None), P("seq", None), P("seq", None)),
        out_specs=(spread,) * 4,
        check_vma=False,
    )


def solution(mesh):
    return build(mesh, GRID, GROUP)
```

```python
import functools

import jax
import jax.numpy as jnp
from jax import lax
from jax.experimental import pallas as pl
from jax.experimental.pallas import tpu as pltpu
from jax.sharding import PartitionSpec as P

HD = 128
BLK = 128
ROWS = 32
GRID = (2, 8, 4)
GROUP = 4
MESH = pl.DeviceIdType.MESH
F32 = jnp.float32
BF16 = jnp.bfloat16
SCALE = HD ** -0.5
EXCLUDED = -1e30


def nt(a, b):
    return lax.dot_general(a, b, (((1,), (1,)), ((), ())), preferred_element_type=F32)


def nn(a, b):
    return lax.dot_general(a, b, (((1,), (0,)), ((), ())), preferred_element_type=F32)


def tn(a, b):
    return lax.dot_general(a, b, (((0,), (0,)), ((), ())), preferred_element_type=F32)


def kernel(
    dims, group, heads,
    q_hbm, k_hbm, v_hbm, w_hbm, index_ref, ct_hbm,
    out_ref,
    w_ref, ct_ref, win, kvg, qdo, bias, wg, stats, osend, orecv, attg, msend, mrecv,
    dqs, dqr, gws, gwr, gs, gy, gzs, gzr, s_ref, dw_ref, seam_a, seam_b,
    local_sem, w_local_sem,
    z_s, z_r, y_s, y_r, win_s, win_r, out_s, in_r, over_s, over_r, last_s, qdo_s, qdo_r, bias_s, bias_r, w_s, w_r,
    st_s, st_r, o_s, o_r, dq_s, dq_r, gy_s, gy_r, gz_s, gz_r, att_s, att_r, mix_s, mix_r,
):
    nz, ny, nx = dims
    count = nz * ny * nx
    groups = heads // group
    seq = lax.axis_index("seq")
    head = lax.axis_index("head")
    z, y, x = seq // (ny * nx), (seq // nx) % ny, seq % nx
    g, r = head // group, head % group

    def at(dz, dy, dx):
        return (((z + dz) % nz * ny + (y + dy) % ny) * nx + (x + dx) % nx, head)

    def member(d):
        return (seq, g * group + (r + d) % group)

    def other_group(e):
        return (seq, (g + e) % groups * group + r)

    following = ((seq + 1) % count, head)
    preceding = ((seq + count - 1) % count, head)

    def send(src, dst, send_sem, recv_sem, device):
        return pltpu.make_async_remote_copy(
            src_ref=src, dst_ref=dst, send_sem=send_sem, recv_sem=recv_sem,
            device_id=device, device_id_type=MESH,
        )

    started, waited = {}, set()

    def start(name, src, dst, send_sem, recv_sem, device):
        copy = send(src, dst, send_sem, recv_sem, device)
        copy.start()
        started[name] = copy

    def received(*name):
        started[name].wait_recv()
        waited.add(name)

    piece = BLK // ny
    is_first = (y == 0) & (x == 0)
    is_last = (y == ny - 1) & (x == nx - 1)
    crossings = (
        (is_last, x == nx - 1, (y + 1) % ny, following, at(0, -y, 1)),
        (is_first, x == 0, y, preceding, at(0, ny - 1 - y, nx - 1)),
    )

    def seam_copy(kind, way, step, t, src, dst, device):
        semaphores = (
            (out_s.at[kind, way, t], in_r.at[kind, way]),
            (over_s.at[kind, way], over_r.at[kind, way]),
            (last_s.at[kind, way], win_r.at[kind, way]),
        )[step]
        return send(src, dst, *semaphores, device)

    def whole(kind, way, src, dst):
        return send(src, dst, win_s.at[kind, way], win_r.at[kind, way], crossings[way][3])

    def scattered(kind, way, src):
        return [
            seam_copy(kind, way, 0, t, src.at[:, t * piece:(t + 1) * piece], seam_a.at[kind, way], at(0, t, 0))
            for t in range(1, ny)
        ]

    def over(kind, way):
        return seam_copy(kind, way, 1, 0, seam_a.at[kind, way], seam_b.at[kind, way], at(1, 0, 0))

    def landing(kind, way, dst):
        rows = pl.ds(pl.multiple_of(crossings[way][2] * piece, piece), piece)
        return seam_copy(kind, way, 2, 0, seam_b.at[kind, way], dst.at[:, rows], crossings[way][4])

    def seam_send(kind, ends):
        for way, (src, dst) in enumerate(ends):
            source = crossings[way][0]

            @pl.when(source)
            def _():
                for copy in scattered(kind, way, src):
                    copy.start()
                seam_a[kind, way] = src[:, :piece]

            @pl.when(jnp.logical_not(source))
            def _():
                whole(kind, way, src, dst).start()

    def seam_over(kind, ends):
        for way in range(2):
            source, column = crossings[way][:2]

            @pl.when(column & jnp.logical_not(source))
            def _():
                scattered(kind, way, ends[way][0])[0].wait_recv()

            @pl.when(column)
            def _():
                over(kind, way).start()

    def seam_land(kind, ends):
        for way in range(2):
            @pl.when(crossings[way][1])
            def _():
                over(kind, way).wait_recv()
                landing(kind, way, ends[way][1]).start()

    def seam_received(kind, ends):
        for way, (src, dst) in enumerate(ends):
            whole(kind, way, src, dst).wait_recv()

    def seam_sent(kind, ends):
        for way, (src, dst) in enumerate(ends):
            source, column = crossings[way][:2]

            @pl.when(source)
            def _():
                for copy in scattered(kind, way, src):
                    copy.wait_send()

            @pl.when(jnp.logical_not(source))
            def _():
                whole(kind, way, src, dst).wait_send()

            @pl.when(column)
            def _():
                over(kind, way).wait_send()
                landing(kind, way, dst).wait_send()

    window_ends = ((win.at[1], win.at[0]), (win.at[1], win.at[2]))
    grad_ends = ((gws.at[1], gwr.at[1]), (gws.at[0], gwr.at[0]))

    partners = [at(1, 0, 0)]
    partners += [at(0, d, 0) for d in range(1, ny)]
    partners += [at(0, 0, d) for d in range(1, nx)]
    partners += [member(d) for d in range(1, group)]
    partners += [other_group(e) for e in range(1, groups)]
    barrier = pltpu.get_barrier_semaphore()

    def greet(device):
        pl.semaphore_signal(barrier, inc=1, device_id=device, device_id_type=MESH)

    for device in partners:
        greet(device)
    for way in range(2):
        @pl.when(jnp.logical_not(crossings[way][0]))
        def _():
            greet(crossings[way][3])

        @pl.when(crossings[1 - way][0])
        def _():
            for t in range(ny):
                greet(at(0, t, 1 if way else nx - 1))

    met = len(partners) + sum(
        jnp.logical_not(source).astype(jnp.int32) + column.astype(jnp.int32)
        for source, column in (c[:2] for c in crossings)
    )

    loads = [
        pltpu.make_async_copy(k_hbm, win.at[1, 0], local_sem.at[0]),
        pltpu.make_async_copy(v_hbm, win.at[1, 1], local_sem.at[1]),
        pltpu.make_async_copy(q_hbm, qdo.at[0, 0], local_sem.at[2]),
        pltpu.make_async_copy(w_hbm, w_ref, local_sem.at[3]),
        pltpu.make_async_copy(ct_hbm, ct_ref, local_sem.at[4]),
    ]
    for load in loads:
        load.start()

    row = lax.broadcasted_iota(jnp.int32, (nz * ny, BLK), 0)
    block = ((z + row // ny) % nz * ny + (y + row % ny) % ny) * nx // (BLK // ROWS)
    listed = jnp.zeros((nz * ny, BLK), F32)
    for slot in range(index_ref.shape[1]):
        listed = listed + (block == index_ref[0, slot]).astype(F32)
    bias[0] = jnp.where(listed > 0, jnp.log(jnp.maximum(listed, 1.0)), EXCLUDED)

    loads[0].wait()
    loads[1].wait()
    kvg[0, 0] = win[1, :, :ROWS, :]
    pl.semaphore_wait(barrier, met)

    start(("z", 0), kvg.at[0, 0], kvg.at[1, 0], z_s.at[0], z_r.at[0], at(1, 0, 0))
    for d in range(1, ny):
        start(("y", 0, d), kvg.at[0, 0], kvg.at[0, ny - d], y_s.at[0, d], y_r.at[0, d], at(0, d, 0))
    seam_send(0, window_ends)
    for d in range(1, nx):
        start(("bias", d), bias.at[0], bias.at[nx - d], bias_s.at[d], bias_r.at[d], at(0, 0, d))

    loads[2].wait()
    loads[3].wait()
    loads[4].wait()
    qdo[0, 1] = nt(ct_ref[...], w_ref[...]).astype(BF16)
    for d in range(1, nx):
        start(("qdo", d), qdo.at[0], qdo.at[nx - d], qdo_s.at[d], qdo_r.at[d], at(0, 0, d))

    received("z", 0)
    for d in range(1, ny):
        start(("y", 1, d), kvg.at[1, 0], kvg.at[1, ny - d], y_s.at[1, d], y_r.at[1, d], at(0, d, 0))

    seam_over(0, window_ends)
    def columns(e, d):
        return pl.ds(pl.multiple_of(((g + e) % groups * group + (r + d) % group) * HD, HD), HD)

    w_loads = []
    for e in range(groups):
        to = pl.ds(e * HD, HD)
        load = pltpu.make_async_copy(w_hbm.at[:, columns(e, 0)], wg.at[0, :, to], w_local_sem.at[e])
        load.start()
        w_loads.append(load)
        for d in range(1, group):
            start(("w", d, e), w_hbm.at[:, columns(e, d)], wg.at[group - d, :, to], w_s.at[d, e], w_r.at[d, e], member(d))

    for d in range(1, nx):
        received("bias", d)
        received("qdo", d)
    queries = qdo[:, 0].reshape(nx * BLK, HD)
    grads = qdo[:, 1].reshape(nx * BLK, HD)
    half = ny * ROWS

    def strided(plane):
        for d in range(1, ny):
            received("y", plane, d)
        rows = pl.ds(plane * half, half)
        keys = kvg[plane, :, 0].reshape(half, HD)
        values = kvg[plane, :, 1].reshape(half, HD)
        s_ref[rows, :] = nt(keys, queries)
        dw_ref[rows, :] = nt(values, grads)

    strided(0)

    seam_land(0, window_ends)
    seam_received(0, window_ends)
    key_w = win[:, 0].reshape(3 * BLK, HD)
    value_w = win[:, 1].reshape(3 * BLK, HD)
    query_own, grad_own = qdo[0, 0], qdo[0, 1]
    score_w = nt(key_w, query_own) * SCALE
    top_w = jnp.max(score_w, axis=0, keepdims=True)
    p_w = jnp.exp(score_w - top_w)
    sum_w = jnp.sum(p_w, axis=0, keepdims=True)
    dw_w = nt(value_w, grad_own)
    delta_w = jnp.sum(p_w * dw_w, axis=0, keepdims=True)
    o_w = tn(value_w, p_w.astype(BF16))

    strided(1)
    chunks = nz * ny
    keys = kvg[:, :, 0].reshape(chunks * ROWS, HD)
    values = kvg[:, :, 1].reshape(chunks * ROWS, HD)
    tops, sums, deltas = [], [], []
    for i in range(nx):
        lanes = pl.ds(i * BLK, BLK)
        spread = jnp.broadcast_to(bias[i][:, None, :], (chunks, ROWS, BLK)).reshape(chunks * ROWS, BLK)
        score = s_ref[:, lanes] * SCALE + spread
        top = jnp.max(score, axis=0, keepdims=True)
        p = jnp.exp(score - top)
        s_ref[:, lanes] = p
        tops.append(top)
        sums.append(jnp.sum(p, axis=0, keepdims=True))
        deltas.append(jnp.sum(p * dw_ref[:, lanes], axis=0, keepdims=True))
    for i in range(nx):
        top, total, delta = tops[i], sums[i], deltas[i]
        if i == 0:
            top = jnp.maximum(tops[0], top_w)
            a, b = jnp.exp(tops[0] - top), jnp.exp(top_w - top)
            total = a * sums[0] + b * sum_w
            delta = a * deltas[0] + b * delta_w
        stats[0, i, 0:1, :] = top
        stats[0, i, 1:2, :] = total
        stats[0, i, 2:3, :] = delta
        stats[0, i, 3:8, :] = jnp.zeros((5, BLK), F32)
    for d in range(1, nx):
        start(("st", d), stats.at[0], stats.at[nx - d], st_s.at[d], st_r.at[d], at(0, 0, d))
    o_part = tn(values, s_ref[...].astype(BF16))
    for d in range(1, nx):
        osend[d] = o_part[:, d * BLK:(d + 1) * BLK].astype(BF16)
        start(("o", d), osend.at[d], orecv.at[nx - d], o_s.at[d], o_r.at[d], at(0, 0, d))
    for d in range(1, nx):
        received("st", d)

    logsums, all_deltas = [], []
    for i in range(nx):
        entries = [(stats[p, (i - p) % nx, 0:1, :], stats[p, (i - p) % nx, 1:2, :], stats[p, (i - p) % nx, 2:3, :]) for p in range(nx)]
        top = functools.reduce(jnp.maximum, [e[0] for e in entries])
        logsum = top + jnp.log(sum(e[1] * jnp.exp(e[0] - top) for e in entries))
        logsums.append(logsum)
        all_deltas.append(sum(e[2] * jnp.exp(e[0] - logsum) for e in entries))

    factor_w = jnp.exp(top_w - logsums[0])
    attention = o_part[:, :BLK] * jnp.exp(tops[0] - logsums[0]) + o_w * factor_w
    for d in range(1, nx):
        p = nx - d
        received("o", d)
        attention = attention + orecv[p].astype(F32) * jnp.exp(stats[p, (-p) % nx, 0:1, :] - logsums[0])
    attg[0] = attention.astype(BF16)
    for d in range(1, group):
        start(("att", d), attg.at[0], attg.at[group - d], att_s.at[d], att_r.at[d], member(d))

    weights, grad_scores = [], []
    for i in range(nx):
        lanes = pl.ds(i * BLK, BLK)
        probability = s_ref[:, lanes] * jnp.exp(tops[i] - logsums[i])
        weights.append(probability.astype(BF16))
        grad_scores.append((probability * (dw_ref[:, lanes] - all_deltas[i]) * SCALE).astype(BF16))
    weights = jnp.concatenate(weights, axis=1)
    grad_scores = jnp.concatenate(grad_scores, axis=1)
    gs[:, :, 0] = nn(grad_scores, queries).astype(BF16).reshape(nz, ny, ROWS, HD)
    gs[:, :, 1] = nn(weights, grads).astype(BF16).reshape(nz, ny, ROWS, HD)
    for plane in (1, 0):
        for d in range(1, ny):
            start(("gy", plane, d), gs.at[plane, d], gy.at[plane, ny - d], gy_s.at[plane, d], gy_r.at[plane, d], at(0, d, 0))

    prob_w = p_w * factor_w
    ds_w = (prob_w * (dw_w - all_deltas[0]) * SCALE).astype(BF16)
    gk_w = nn(ds_w, query_own)
    gv_w = nn(prob_w.astype(BF16), grad_own)
    gws[0, 0] = gk_w[:BLK].astype(BF16)
    gws[0, 1] = gv_w[:BLK].astype(BF16)
    gws[1, 0] = gk_w[2 * BLK:].astype(BF16)
    gws[1, 1] = gv_w[2 * BLK:].astype(BF16)
    seam_send(1, grad_ends)

    dq = tn(keys, grad_scores)
    for d in range(1, nx):
        dqs[d] = dq[:, d * BLK:(d + 1) * BLK].astype(BF16)
        start(("dq", d), dqs.at[d], dqr.at[nx - d], dq_s.at[d], dq_r.at[d], at(0, 0, d))
    dq_own = dq[:, :BLK] + tn(key_w, ds_w)

    seam_over(1, grad_ends)
    for load in w_loads:
        load.wait()
    for d in range(1, group):
        for e in range(groups):
            received("w", d, e)
        received("att", d)
    mixed = tn(attg[...].reshape(group * HD, BLK), wg[...].reshape(group * HD, groups * HD))
    for e in range(1, groups):
        msend[e] = mixed[:, e * HD:(e + 1) * HD].astype(BF16)
        start(("mix", e), msend.at[e], mrecv.at[groups - e], mix_s.at[e], mix_r.at[e], other_group(e))
    mixed_own = mixed[:, :HD]

    seam_land(1, grad_ends)
    total = gs[1, 0].astype(F32)
    for d in range(1, ny):
        received("gy", 1, d)
        total = total + gy[1, ny - d].astype(F32)
    gzs[...] = total.astype(BF16)
    start(("gz", 0), gzs, gzr, gz_s.at[0], gz_r.at[0], at(1, 0, 0))

    for d in range(1, nx):
        received("dq", d)
        dq_own = dq_own + dqr[nx - d].astype(F32)
    out_ref[1] = dq_own.T.astype(BF16)

    seam_received(1, grad_ends)
    own_k = gk_w[BLK:2 * BLK] + gwr[0, 0].astype(F32) + gwr[1, 0].astype(F32)
    own_v = gv_w[BLK:2 * BLK] + gwr[0, 1].astype(F32) + gwr[1, 1].astype(F32)
    out_ref[2, ROWS:, :] = own_k[ROWS:].astype(BF16)
    out_ref[3, ROWS:, :] = own_v[ROWS:].astype(BF16)

    total = gs[0, 0].astype(F32)
    for d in range(1, ny):
        received("gy", 0, d)
        total = total + gy[0, ny - d].astype(F32)

    for e in range(1, groups):
        received("mix", e)
        mixed_own = mixed_own + mrecv[groups - e].astype(F32)
    out_ref[0] = mixed_own.astype(BF16)

    received("gz", 0)
    total = total + gzr[...].astype(F32)
    out_ref[2, :ROWS, :] = (own_k[:ROWS] + total[0]).astype(BF16)
    out_ref[3, :ROWS, :] = (own_v[:ROWS] + total[1]).astype(BF16)

    for copy in started.values():
        copy.wait_send()
    seam_sent(0, window_ends)
    seam_sent(1, grad_ends)


def build(mesh, dims, group):
    nz, ny, nx = dims
    heads = mesh.shape["head"]
    groups = heads // group
    chunks = nz * ny

    def shards(queries, key_rows, value_rows, out_weight, strided_index, cotangent):
        width = out_weight.shape[1]
        dma = pltpu.SemaphoreType.DMA
        hbm = pl.BlockSpec(memory_space=pl.ANY)
        vmem = pl.BlockSpec(memory_space=pltpu.VMEM)
        square = lambda n: pltpu.VMEM((n, BLK, HD), BF16)
        pieces = lambda: pltpu.VMEM((nz, ny, 2, ROWS, HD), BF16)
        out = pl.pallas_call(
            functools.partial(kernel, dims, group, heads),
            out_shape=jax.ShapeDtypeStruct((4, BLK, HD), BF16),
            in_specs=[hbm, hbm, hbm, hbm, pl.BlockSpec(memory_space=pltpu.SMEM), hbm],
            out_specs=vmem,
            scratch_shapes=[
                pltpu.VMEM((HD, width), BF16),
                pltpu.VMEM((BLK, width), BF16),
                pltpu.VMEM((3, 2, BLK, HD), BF16),
                pieces(),
                pltpu.VMEM((nx, 2, BLK, HD), BF16),
                pltpu.VMEM((nx, chunks, BLK), F32),
                pltpu.VMEM((group, HD, groups * HD), BF16),
                pltpu.VMEM((nx, nx, 8, BLK), F32),
                square(nx), square(nx),
                square(group),
                square(groups), square(groups),
                square(nx), square(nx),
                pltpu.VMEM((2, 2, BLK, HD), BF16), pltpu.VMEM((2, 2, BLK, HD), BF16),
                pieces(), pieces(),
                pltpu.VMEM((2, ROWS, HD), BF16), pltpu.VMEM((2, ROWS, HD), BF16),
                pltpu.VMEM((chunks * ROWS, nx * BLK), F32),
                pltpu.VMEM((chunks * ROWS, nx * BLK), F32),
                pltpu.VMEM((2, 2, 2, BLK // ny, HD), BF16), pltpu.VMEM((2, 2, 2, BLK // ny, HD), BF16),
                dma((5,)), dma((groups,)),
                dma((1,)), dma((1,)),
                dma((2, ny)), dma((2, ny)),
                dma((2, 2)), dma((2, 2)),
                dma((2, 2, ny)), dma((2, 2)), dma((2, 2)), dma((2, 2)), dma((2, 2)),
                dma((nx,)), dma((nx,)),
                dma((nx,)), dma((nx,)),
                dma((group, groups)), dma((group, groups)),
                dma((nx,)), dma((nx,)),
                dma((nx,)), dma((nx,)),
                dma((nx,)), dma((nx,)),
                dma((2, ny)), dma((2, ny)),
                dma((1,)), dma((1,)),
                dma((group,)), dma((group,)),
                dma((groups,)), dma((groups,)),
            ],
            compiler_params=pltpu.CompilerParams(
                collective_id=0, has_side_effects=True, vmem_limit_bytes=56 * 2 ** 20
            ),
        )(queries, key_rows, value_rows, out_weight, strided_index, cotangent)
        return tuple(out[i] for i in range(4))

    spread = P("seq", "head")
    return jax.shard_map(
        shards,
        mesh=mesh,
        in_specs=(spread, spread, spread, P("head", None), P("seq", None), P("seq", None)),
        out_specs=(spread,) * 4,
        check_vma=False,
    )


def solution(mesh):
    return build(mesh, GRID, GROUP)
```

```python
import functools

import jax
import jax.numpy as jnp
from jax import lax
from jax.experimental import pallas as pl
from jax.experimental.pallas import tpu as pltpu
from jax.sharding import PartitionSpec as P

HD = 128
BLK = 128
ROWS = 32
GRID = (2, 8, 4)
GROUP = 4
MESH = pl.DeviceIdType.MESH
F32 = jnp.float32
BF16 = jnp.bfloat16
SCALE = HD ** -0.5
EXCLUDED = -1e30


def nt(a, b):
    return lax.dot_general(a, b, (((1,), (1,)), ((), ())), preferred_element_type=F32)


def nn(a, b):
    return lax.dot_general(a, b, (((1,), (0,)), ((), ())), preferred_element_type=F32)


def tn(a, b):
    return lax.dot_general(a, b, (((0,), (0,)), ((), ())), preferred_element_type=F32)


def kernel(
    dims, group, heads,
    q_hbm, k_hbm, v_hbm, w_hbm, index_ref, ct_hbm,
    out_ref,
    w_ref, ct_ref, win, kvg, qdo, bias, wg, stats, osend, orecv, attg, msend, mrecv,
    dqs, dqr, gws, gwr, gs, gy, gzs, gzr, s_ref, dw_ref, seam_a, seam_b,
    local_sem, w_local_sem,
    z_s, z_r, y_s, y_r, win_s, win_r, out_s, in_r, over_s, over_r, last_s, qdo_s, qdo_r, bias_s, bias_r, w_s, w_r,
    st_s, st_r, o_s, o_r, dq_s, dq_r, gy_s, gy_r, gz_s, gz_r, att_s, att_r, mix_s, mix_r,
):
    nz, ny, nx = dims
    groups = heads // group
    seq = lax.axis_index("seq")
    head = lax.axis_index("head")
    z, y, x = seq // (ny * nx), (seq // nx) % ny, seq % nx
    g, r = head // group, head % group

    def at(dz, dy, dx):
        return (((z + dz) % nz * ny + (y + dy) % ny) * nx + (x + dx) % nx, head)

    def member(d):
        return (seq, g * group + (r + d) % group)

    def other_group(e):
        return (seq, (g + e) % groups * group + r)

    plane = ny * nx
    place = seq % plane
    following = (z * plane + (place + 1) % plane, head)
    preceding = (z * plane + (place + plane - 1) % plane, head)

    def send(src, dst, send_sem, recv_sem, device):
        return pltpu.make_async_remote_copy(
            src_ref=src, dst_ref=dst, send_sem=send_sem, recv_sem=recv_sem,
            device_id=device, device_id_type=MESH,
        )

    started, waited = {}, set()

    def start(name, src, dst, send_sem, recv_sem, device):
        copy = send(src, dst, send_sem, recv_sem, device)
        copy.start()
        started[name] = copy

    def received(*name):
        started[name].wait_recv()
        waited.add(name)

    pieces, piece = 4, BLK // 4
    is_last = (y == ny - 1) & (x == nx - 1)
    is_first = (y == 0) & (x == 0)
    corner = ((y == 0) | (y == ny - 1)) & ((x == 0) | (x == nx - 1))
    low = (y == 0).astype(jnp.int32) + 2 * (x == 0).astype(jnp.int32)
    ways = (
        (is_last, 1, following, low, at(0, -y, -x)),
        (is_first, -1, preceding, 3 - low, at(0, ny - 1 - y, nx - 1 - x)),
    )

    def whole(kind, way, src, dst):
        return send(src, dst, win_s.at[kind, way], win_r.at[kind, way], ways[way][2])

    def scattered(kind, way, src):
        step = ways[way][1]
        return [
            send(src.at[:, t * piece:(t + 1) * piece], seam_a.at[kind, way], out_s.at[kind, way, t], in_r.at[kind, way], at(0, step * (t & 1), step * (t >> 1)))
            for t in range(1, pieces)
        ]

    def over(kind, way):
        return send(seam_a.at[kind, way], seam_b.at[kind, way], over_s.at[kind, way], over_r.at[kind, way], at(1, 0, 0))

    def over_last(kind, way, dst):
        return send(seam_a.at[kind, way], dst.at[:, (pieces - 1) * piece:], over_s.at[kind, way], win_r.at[kind, way], at(1, 0, 0))

    def landing(kind, way, dst):
        rows = pl.ds(pl.multiple_of(ways[way][3] * piece, piece), piece)
        return send(seam_b.at[kind, way], dst.at[:, rows], last_s.at[kind, way], win_r.at[kind, way], ways[way][4])

    def seam_send(kind, ends):
        for way, (src, dst) in enumerate(ends):
            source = ways[way][0]

            @pl.when(source)
            def _():
                for copy in scattered(kind, way, src):
                    copy.start()
                seam_a[kind, way] = src[:, :piece]

            @pl.when(jnp.logical_not(source))
            def _():
                whole(kind, way, src, dst).start()

    def seam_over(kind, ends):
        for way, (src, dst) in enumerate(ends):
            number = ways[way][3]

            @pl.when(corner & (number > 0))
            def _():
                scattered(kind, way, src)[0].wait_recv()

            @pl.when(corner & (number < pieces - 1))
            def _():
                over(kind, way).start()

            @pl.when(corner & (number == pieces - 1))
            def _():
                over_last(kind, way, dst).start()

    def seam_land(kind, ends):
        for way, (src, dst) in enumerate(ends):
            @pl.when(corner & (ways[way][3] < pieces - 1))
            def _():
                over(kind, way).wait_recv()
                landing(kind, way, dst).start()

    def seam_received(kind, ends):
        for way, (src, dst) in enumerate(ends):
            whole(kind, way, src, dst).wait_recv()

    def seam_sent(kind, ends):
        for way, (src, dst) in enumerate(ends):
            source, number = ways[way][0], ways[way][3]

            @pl.when(source)
            def _():
                for copy in scattered(kind, way, src):
                    copy.wait_send()

            @pl.when(jnp.logical_not(source))
            def _():
                whole(kind, way, src, dst).wait_send()

            @pl.when(corner)
            def _():
                over(kind, way).wait_send()

            @pl.when(corner & (number < pieces - 1))
            def _():
                landing(kind, way, dst).wait_send()

    window_ends = ((win.at[1], win.at[0]), (win.at[1], win.at[2]))
    grad_ends = ((gws.at[1], gwr.at[1]), (gws.at[0], gwr.at[0]))

    partners = [at(1, 0, 0)]
    partners += [at(0, d, 0) for d in range(1, ny)]
    partners += [at(0, 0, d) for d in range(1, nx)]
    partners += [following, preceding]
    partners += [member(d) for d in range(1, group)]
    partners += [other_group(e) for e in range(1, groups)]
    barrier = pltpu.get_barrier_semaphore()

    for device in partners:
        pl.semaphore_signal(barrier, inc=1, device_id=device, device_id_type=MESH)

    loads = [
        pltpu.make_async_copy(k_hbm, win.at[1, 0], local_sem.at[0]),
        pltpu.make_async_copy(v_hbm, win.at[1, 1], local_sem.at[1]),
        pltpu.make_async_copy(q_hbm, qdo.at[0, 0], local_sem.at[2]),
        pltpu.make_async_copy(w_hbm, w_ref, local_sem.at[3]),
        pltpu.make_async_copy(ct_hbm, ct_ref, local_sem.at[4]),
    ]
    for load in loads:
        load.start()

    row = lax.broadcasted_iota(jnp.int32, (nz * ny, BLK), 0)
    block = ((z + row // ny) % nz * ny + (y + row % ny) % ny) * nx // (BLK // ROWS)
    listed = jnp.zeros((nz * ny, BLK), F32)
    for slot in range(index_ref.shape[1]):
        listed = listed + (block == index_ref[0, slot]).astype(F32)
    bias[0] = jnp.where(listed > 0, jnp.log(jnp.maximum(listed, 1.0)), EXCLUDED)

    loads[0].wait()
    loads[1].wait()
    kvg[0, 0] = win[1, :, :ROWS, :]
    pl.semaphore_wait(barrier, len(partners))

    start(("z", 0), kvg.at[0, 0], kvg.at[1, 0], z_s.at[0], z_r.at[0], at(1, 0, 0))
    for d in range(1, ny):
        start(("y", 0, d), kvg.at[0, 0], kvg.at[0, ny - d], y_s.at[0, d], y_r.at[0, d], at(0, d, 0))
    seam_send(0, window_ends)
    for d in range(1, nx):
        start(("bias", d), bias.at[0], bias.at[nx - d], bias_s.at[d], bias_r.at[d], at(0, 0, d))

    loads[2].wait()
    loads[3].wait()
    loads[4].wait()
    qdo[0, 1] = nt(ct_ref[...], w_ref[...]).astype(BF16)
    for d in range(1, nx):
        start(("qdo", d), qdo.at[0], qdo.at[nx - d], qdo_s.at[d], qdo_r.at[d], at(0, 0, d))

    seam_over(0, window_ends)
    def columns(e, d):
        return pl.ds(pl.multiple_of(((g + e) % groups * group + (r + d) % group) * HD, HD), HD)

    w_loads = []
    for e in range(groups):
        to = pl.ds(e * HD, HD)
        load = pltpu.make_async_copy(w_hbm.at[:, columns(e, 0)], wg.at[0, :, to], w_local_sem.at[e])
        load.start()
        w_loads.append(load)
        for d in range(1, group):
            start(("w", d, e), w_hbm.at[:, columns(e, d)], wg.at[group - d, :, to], w_s.at[d, e], w_r.at[d, e], member(d))

    for d in range(1, nx):
        received("bias", d)
        received("qdo", d)
    queries = qdo[:, 0].reshape(nx * BLK, HD)
    grads = qdo[:, 1].reshape(nx * BLK, HD)
    half = ny * ROWS

    def strided(plane):
        for d in range(1, ny):
            received("y", plane, d)
        rows = pl.ds(plane * half, half)
        keys = kvg[plane, :, 0].reshape(half, HD)
        values = kvg[plane, :, 1].reshape(half, HD)
        s_ref[rows, :] = nt(keys, queries)
        dw_ref[rows, :] = nt(values, grads)

    strided(0)

    received("z", 0)
    for d in range(1, ny):
        start(("y", 1, d), kvg.at[1, 0], kvg.at[1, ny - d], y_s.at[1, d], y_r.at[1, d], at(0, d, 0))


    seam_land(0, window_ends)
    seam_received(0, window_ends)
    key_w = win[:, 0].reshape(3 * BLK, HD)
    value_w = win[:, 1].reshape(3 * BLK, HD)
    query_own, grad_own = qdo[0, 0], qdo[0, 1]
    score_w = nt(key_w, query_own) * SCALE
    top_w = jnp.max(score_w, axis=0, keepdims=True)
    p_w = jnp.exp(score_w - top_w)
    sum_w = jnp.sum(p_w, axis=0, keepdims=True)
    dw_w = nt(value_w, grad_own)
    delta_w = jnp.sum(p_w * dw_w, axis=0, keepdims=True)
    o_w = tn(value_w, p_w.astype(BF16))

    strided(1)
    chunks = nz * ny
    keys = kvg[:, :, 0].reshape(chunks * ROWS, HD)
    values = kvg[:, :, 1].reshape(chunks * ROWS, HD)
    tops, sums, deltas = [], [], []
    for i in range(nx):
        lanes = pl.ds(i * BLK, BLK)
        spread = jnp.broadcast_to(bias[i][:, None, :], (chunks, ROWS, BLK)).reshape(chunks * ROWS, BLK)
        score = s_ref[:, lanes] * SCALE + spread
        top = jnp.max(score, axis=0, keepdims=True)
        p = jnp.exp(score - top)
        s_ref[:, lanes] = p
        tops.append(top)
        sums.append(jnp.sum(p, axis=0, keepdims=True))
        deltas.append(jnp.sum(p * dw_ref[:, lanes], axis=0, keepdims=True))
    for i in range(nx):
        top, total, delta = tops[i], sums[i], deltas[i]
        if i == 0:
            top = jnp.maximum(tops[0], top_w)
            a, b = jnp.exp(tops[0] - top), jnp.exp(top_w - top)
            total = a * sums[0] + b * sum_w
            delta = a * deltas[0] + b * delta_w
        stats[0, i, 0:1, :] = top
        stats[0, i, 1:2, :] = total
        stats[0, i, 2:3, :] = delta
        stats[0, i, 3:8, :] = jnp.zeros((5, BLK), F32)
    for d in range(1, nx):
        start(("st", d), stats.at[0], stats.at[nx - d], st_s.at[d], st_r.at[d], at(0, 0, d))
    o_part = tn(values, s_ref[...].astype(BF16))
    for d in range(1, nx):
        osend[d] = o_part[:, d * BLK:(d + 1) * BLK].astype(BF16)
        start(("o", d), osend.at[d], orecv.at[nx - d], o_s.at[d], o_r.at[d], at(0, 0, d))
    for d in range(1, nx):
        received("st", d)

    logsums, all_deltas = [], []
    for i in range(nx):
        entries = [(stats[p, (i - p) % nx, 0:1, :], stats[p, (i - p) % nx, 1:2, :], stats[p, (i - p) % nx, 2:3, :]) for p in range(nx)]
        top = functools.reduce(jnp.maximum, [e[0] for e in entries])
        logsum = top + jnp.log(sum(e[1] * jnp.exp(e[0] - top) for e in entries))
        logsums.append(logsum)
        all_deltas.append(sum(e[2] * jnp.exp(e[0] - logsum) for e in entries))

    factor_w = jnp.exp(top_w - logsums[0])
    attention = o_part[:, :BLK] * jnp.exp(tops[0] - logsums[0]) + o_w * factor_w
    for d in range(1, nx):
        p = nx - d
        received("o", d)
        attention = attention + orecv[p].astype(F32) * jnp.exp(stats[p, (-p) % nx, 0:1, :] - logsums[0])
    attg[0] = attention.astype(BF16)
    for d in range(1, group):
        start(("att", d), attg.at[0], attg.at[group - d], att_s.at[d], att_r.at[d], member(d))

    weights, grad_scores = [], []
    for i in range(nx):
        lanes = pl.ds(i * BLK, BLK)
        probability = s_ref[:, lanes] * jnp.exp(tops[i] - logsums[i])
        weights.append(probability.astype(BF16))
        grad_scores.append((probability * (dw_ref[:, lanes] - all_deltas[i]) * SCALE).astype(BF16))
    weights = jnp.concatenate(weights, axis=1)
    grad_scores = jnp.concatenate(grad_scores, axis=1)
    gs[:, :, 0] = nn(grad_scores, queries).astype(BF16).reshape(nz, ny, ROWS, HD)
    gs[:, :, 1] = nn(weights, grads).astype(BF16).reshape(nz, ny, ROWS, HD)
    for half_index in (1, 0):
        for d in range(1, ny):
            start(("gy", half_index, d), gs.at[half_index, d], gy.at[half_index, ny - d], gy_s.at[half_index, d], gy_r.at[half_index, d], at(0, d, 0))

    prob_w = p_w * factor_w
    ds_w = (prob_w * (dw_w - all_deltas[0]) * SCALE).astype(BF16)
    gk_w = nn(ds_w, query_own)
    gv_w = nn(prob_w.astype(BF16), grad_own)
    gws[0, 0] = gk_w[:BLK].astype(BF16)
    gws[0, 1] = gv_w[:BLK].astype(BF16)
    gws[1, 0] = gk_w[2 * BLK:].astype(BF16)
    gws[1, 1] = gv_w[2 * BLK:].astype(BF16)
    seam_send(1, grad_ends)

    dq = tn(keys, grad_scores)
    for d in range(1, nx):
        dqs[d] = dq[:, d * BLK:(d + 1) * BLK].astype(BF16)
        start(("dq", d), dqs.at[d], dqr.at[nx - d], dq_s.at[d], dq_r.at[d], at(0, 0, d))
    dq_own = dq[:, :BLK] + tn(key_w, ds_w)

    seam_over(1, grad_ends)
    for load in w_loads:
        load.wait()
    for d in range(1, group):
        for e in range(groups):
            received("w", d, e)
        received("att", d)
    mixed = tn(attg[...].reshape(group * HD, BLK), wg[...].reshape(group * HD, groups * HD))
    for e in range(1, groups):
        msend[e] = mixed[:, e * HD:(e + 1) * HD].astype(BF16)
        start(("mix", e), msend.at[e], mrecv.at[groups - e], mix_s.at[e], mix_r.at[e], other_group(e))
    mixed_own = mixed[:, :HD]

    seam_land(1, grad_ends)
    total = gs[1, 0].astype(F32)
    for d in range(1, ny):
        received("gy", 1, d)
        total = total + gy[1, ny - d].astype(F32)
    gzs[...] = total.astype(BF16)
    start(("gz", 0), gzs, gzr, gz_s.at[0], gz_r.at[0], at(1, 0, 0))

    for d in range(1, nx):
        received("dq", d)
        dq_own = dq_own + dqr[nx - d].astype(F32)
    out_ref[1] = dq_own.T.astype(BF16)

    seam_received(1, grad_ends)
    own_k = gk_w[BLK:2 * BLK] + gwr[0, 0].astype(F32) + gwr[1, 0].astype(F32)
    own_v = gv_w[BLK:2 * BLK] + gwr[0, 1].astype(F32) + gwr[1, 1].astype(F32)
    out_ref[2, ROWS:, :] = own_k[ROWS:].astype(BF16)
    out_ref[3, ROWS:, :] = own_v[ROWS:].astype(BF16)

    total = gs[0, 0].astype(F32)
    for d in range(1, ny):
        received("gy", 0, d)
        total = total + gy[0, ny - d].astype(F32)

    for e in range(1, groups):
        received("mix", e)
        mixed_own = mixed_own + mrecv[groups - e].astype(F32)
    out_ref[0] = mixed_own.astype(BF16)

    received("gz", 0)
    total = total + gzr[...].astype(F32)
    out_ref[2, :ROWS, :] = (own_k[:ROWS] + total[0]).astype(BF16)
    out_ref[3, :ROWS, :] = (own_v[:ROWS] + total[1]).astype(BF16)

    for copy in started.values():
        copy.wait_send()
    seam_sent(0, window_ends)
    seam_sent(1, grad_ends)


def build(mesh, dims, group):
    nz, ny, nx = dims
    heads = mesh.shape["head"]
    groups = heads // group
    chunks = nz * ny

    def shards(queries, key_rows, value_rows, out_weight, strided_index, cotangent):
        width = out_weight.shape[1]
        dma = pltpu.SemaphoreType.DMA
        hbm = pl.BlockSpec(memory_space=pl.ANY)
        vmem = pl.BlockSpec(memory_space=pltpu.VMEM)
        square = lambda n: pltpu.VMEM((n, BLK, HD), BF16)
        pieces = lambda: pltpu.VMEM((nz, ny, 2, ROWS, HD), BF16)
        out = pl.pallas_call(
            functools.partial(kernel, dims, group, heads),
            out_shape=jax.ShapeDtypeStruct((4, BLK, HD), BF16),
            in_specs=[hbm, hbm, hbm, hbm, pl.BlockSpec(memory_space=pltpu.SMEM), hbm],
            out_specs=vmem,
            scratch_shapes=[
                pltpu.VMEM((HD, width), BF16),
                pltpu.VMEM((BLK, width), BF16),
                pltpu.VMEM((3, 2, BLK, HD), BF16),
                pieces(),
                pltpu.VMEM((nx, 2, BLK, HD), BF16),
                pltpu.VMEM((nx, chunks, BLK), F32),
                pltpu.VMEM((group, HD, groups * HD), BF16),
                pltpu.VMEM((nx, nx, 8, BLK), F32),
                square(nx), square(nx),
                square(group),
                square(groups), square(groups),
                square(nx), square(nx),
                pltpu.VMEM((2, 2, BLK, HD), BF16), pltpu.VMEM((2, 2, BLK, HD), BF16),
                pieces(), pieces(),
                pltpu.VMEM((2, ROWS, HD), BF16), pltpu.VMEM((2, ROWS, HD), BF16),
                pltpu.VMEM((chunks * ROWS, nx * BLK), F32),
                pltpu.VMEM((chunks * ROWS, nx * BLK), F32),
                pltpu.VMEM((2, 2, 2, BLK // 4, HD), BF16), pltpu.VMEM((2, 2, 2, BLK // 4, HD), BF16),
                dma((5,)), dma((groups,)),
                dma((1,)), dma((1,)),
                dma((2, ny)), dma((2, ny)),
                dma((2, 2)), dma((2, 2)),
                dma((2, 2, 4)), dma((2, 2)), dma((2, 2)), dma((2, 2)), dma((2, 2)),
                dma((nx,)), dma((nx,)),
                dma((nx,)), dma((nx,)),
                dma((group, groups)), dma((group, groups)),
                dma((nx,)), dma((nx,)),
                dma((nx,)), dma((nx,)),
                dma((nx,)), dma((nx,)),
                dma((2, ny)), dma((2, ny)),
                dma((1,)), dma((1,)),
                dma((group,)), dma((group,)),
                dma((groups,)), dma((groups,)),
            ],
            compiler_params=pltpu.CompilerParams(
                collective_id=0, has_side_effects=True, vmem_limit_bytes=56 * 2 ** 20
            ),
        )(queries, key_rows, value_rows, out_weight, strided_index, cotangent)
        return tuple(out[i] for i in range(4))

    spread = P("seq", "head")
    return jax.shard_map(
        shards,
        mesh=mesh,
        in_specs=(spread, spread, spread, P("head", None), P("seq", None), P("seq", None)),
        out_specs=(spread,) * 4,
        check_vma=False,
    )


def solution(mesh):
    return build(mesh, GRID, GROUP)
```

```python
import functools

import jax
import jax.numpy as jnp
from jax import lax
from jax.experimental import pallas as pl
from jax.experimental.pallas import tpu as pltpu
from jax.sharding import PartitionSpec as P

HD = 128
BLK = 128
ROWS = 32
GRID = (2, 8, 4)
GROUP = 4
MESH = pl.DeviceIdType.MESH
F32 = jnp.float32
BF16 = jnp.bfloat16
SCALE = HD ** -0.5
EXCLUDED = -1e30


def nt(a, b):
    return lax.dot_general(a, b, (((1,), (1,)), ((), ())), preferred_element_type=F32)


def nn(a, b):
    return lax.dot_general(a, b, (((1,), (0,)), ((), ())), preferred_element_type=F32)


def tn(a, b):
    return lax.dot_general(a, b, (((0,), (0,)), ((), ())), preferred_element_type=F32)


def kernel(
    dims, group, heads,
    q_hbm, k_hbm, v_hbm, w_hbm, index_ref, ct_hbm,
    out_ref,
    w_ref, ct_ref, win, kvg, qdo, bias, wg, stats, osend, orecv, attg, msend, mrecv,
    dqs, dqr, near, own_rows, near_rows, relay_rows, gs, gy, gzs, gzr, s_ref, dw_ref, seam_a, seam_b,
    local_sem, w_local_sem,
    z_s, z_r, y_s, y_r, win_s, win_r, out_s, in_r, over_s, over_r, last_s, row_s, row_r, relay_s, relay_r, qdo_s, qdo_r, bias_s, bias_r, w_s, w_r,
    st_s, st_r, o_s, o_r, dq_s, dq_r, gy_s, gy_r, gz_s, gz_r, att_s, att_r, mix_s, mix_r,
):
    nz, ny, nx = dims
    groups = heads // group
    seq = lax.axis_index("seq")
    head = lax.axis_index("head")
    z, y, x = seq // (ny * nx), (seq // nx) % ny, seq % nx
    g, r = head // group, head % group

    def at(dz, dy, dx):
        return (((z + dz) % nz * ny + (y + dy) % ny) * nx + (x + dx) % nx, head)

    def member(d):
        return (seq, g * group + (r + d) % group)

    def other_group(e):
        return (seq, (g + e) % groups * group + r)

    plane = ny * nx
    place = seq % plane
    following = (z * plane + (place + 1) % plane, head)
    preceding = (z * plane + (place + plane - 1) % plane, head)

    def send(src, dst, send_sem, recv_sem, device):
        return pltpu.make_async_remote_copy(
            src_ref=src, dst_ref=dst, send_sem=send_sem, recv_sem=recv_sem,
            device_id=device, device_id_type=MESH,
        )

    started, waited = {}, set()

    def start(name, src, dst, send_sem, recv_sem, device):
        copy = send(src, dst, send_sem, recv_sem, device)
        copy.start()
        started[name] = copy

    def received(*name):
        started[name].wait_recv()
        waited.add(name)

    pieces, piece = 4, BLK // 4
    is_last = (y == ny - 1) & (x == nx - 1)
    is_first = (y == 0) & (x == 0)
    corner = ((y == 0) | (y == ny - 1)) & ((x == 0) | (x == nx - 1))
    low = (y == 0).astype(jnp.int32) + 2 * (x == 0).astype(jnp.int32)
    ways = (
        (is_last, 1, following, low, at(0, -y, -x)),
        (is_first, -1, preceding, 3 - low, at(0, ny - 1 - y, nx - 1 - x)),
    )

    def whole(kind, way, src, dst):
        return send(src, dst, win_s.at[kind, way], win_r.at[kind, way], ways[way][2])

    def scattered(kind, way, src):
        step = ways[way][1]
        return [
            send(src.at[:, t * piece:(t + 1) * piece], seam_a.at[kind, way], out_s.at[kind, way, t], in_r.at[kind, way], at(0, step * (t & 1), step * (t >> 1)))
            for t in range(1, pieces)
        ]

    def over(kind, way):
        return send(seam_a.at[kind, way], seam_b.at[kind, way], over_s.at[kind, way], over_r.at[kind, way], at(1, 0, 0))

    def over_last(kind, way, dst):
        return send(seam_a.at[kind, way], dst.at[:, (pieces - 1) * piece:], over_s.at[kind, way], win_r.at[kind, way], at(1, 0, 0))

    def landing(kind, way, dst):
        rows = pl.ds(pl.multiple_of(ways[way][3] * piece, piece), piece)
        return send(seam_b.at[kind, way], dst.at[:, rows], last_s.at[kind, way], win_r.at[kind, way], ways[way][4])

    def seam_send(kind, ends):
        for way, (src, dst) in enumerate(ends):
            source = ways[way][0]

            @pl.when(source)
            def _():
                for copy in scattered(kind, way, src):
                    copy.start()
                seam_a[kind, way] = src[:, :piece]

            @pl.when(jnp.logical_not(source))
            def _():
                whole(kind, way, src, dst).start()

    def seam_over(kind, ends):
        for way, (src, dst) in enumerate(ends):
            number = ways[way][3]

            @pl.when(corner & (number > 0))
            def _():
                scattered(kind, way, src)[0].wait_recv()

            @pl.when(corner & (number < pieces - 1))
            def _():
                over(kind, way).start()

            @pl.when(corner & (number == pieces - 1))
            def _():
                over_last(kind, way, dst).start()

    def seam_land(kind, ends):
        for way, (src, dst) in enumerate(ends):
            @pl.when(corner & (ways[way][3] < pieces - 1))
            def _():
                over(kind, way).wait_recv()
                landing(kind, way, dst).start()

    def seam_received(kind, ends):
        for way, (src, dst) in enumerate(ends):
            whole(kind, way, src, dst).wait_recv()

    def seam_sent(kind, ends):
        for way, (src, dst) in enumerate(ends):
            source, number = ways[way][0], ways[way][3]

            @pl.when(source)
            def _():
                for copy in scattered(kind, way, src):
                    copy.wait_send()

            @pl.when(jnp.logical_not(source))
            def _():
                whole(kind, way, src, dst).wait_send()

            @pl.when(corner)
            def _():
                over(kind, way).wait_send()

            @pl.when(corner & (number < pieces - 1))
            def _():
                landing(kind, way, dst).wait_send()

    def row_copy(way, source):
        to, arrived = (relay_rows.at[way], relay_r.at[way]) if source else (near_rows.at[way], row_r.at[way])
        return send(own_rows, to, row_s.at[way], arrived, ways[way][2])

    def row_relay(way):
        return send(relay_rows.at[way], near_rows.at[way], relay_s.at[way], row_r.at[way], at(1, 0, 0))

    def either(way, action):
        for source in (True, False):
            @pl.when(ways[way][0] == source)
            def _():
                action(row_copy(way, source))

    window_ends = ((win.at[1], win.at[0]), (win.at[1], win.at[2]))
    query_ends = ((qdo.at[0], near.at[0]), (qdo.at[0], near.at[1]))

    partners = [at(1, 0, 0)]
    partners += [at(0, d, 0) for d in range(1, ny)]
    partners += [at(0, 0, d) for d in range(1, nx)]
    partners += [following, preceding]
    partners += [member(d) for d in range(1, group)]
    partners += [other_group(e) for e in range(1, groups)]
    barrier = pltpu.get_barrier_semaphore()

    for device in partners:
        pl.semaphore_signal(barrier, inc=1, device_id=device, device_id_type=MESH)

    loads = [
        pltpu.make_async_copy(k_hbm, win.at[1, 0], local_sem.at[0]),
        pltpu.make_async_copy(v_hbm, win.at[1, 1], local_sem.at[1]),
        pltpu.make_async_copy(q_hbm, qdo.at[0, 0], local_sem.at[2]),
        pltpu.make_async_copy(w_hbm, w_ref, local_sem.at[3]),
        pltpu.make_async_copy(ct_hbm, ct_ref, local_sem.at[4]),
    ]
    for load in loads:
        load.start()

    row = lax.broadcasted_iota(jnp.int32, (nz * ny, BLK), 0)
    block = ((z + row // ny) % nz * ny + (y + row % ny) % ny) * nx // (BLK // ROWS)
    listed = jnp.zeros((nz * ny, BLK), F32)
    for slot in range(index_ref.shape[1]):
        listed = listed + (block == index_ref[0, slot]).astype(F32)
    bias[0] = jnp.where(listed > 0, jnp.log(jnp.maximum(listed, 1.0)), EXCLUDED)

    loads[0].wait()
    loads[1].wait()
    kvg[0, 0] = win[1, :, :ROWS, :]
    loads[2].wait()
    loads[3].wait()
    loads[4].wait()
    qdo[0, 1] = nt(ct_ref[...], w_ref[...]).astype(BF16)
    pl.semaphore_wait(barrier, len(partners))

    seam_send(0, window_ends)
    start(("z", 0), kvg.at[0, 0], kvg.at[1, 0], z_s.at[0], z_r.at[0], at(1, 0, 0))
    for d in range(1, ny):
        start(("y", 0, d), kvg.at[0, 0], kvg.at[0, ny - d], y_s.at[0, d], y_r.at[0, d], at(0, d, 0))
    for d in range(1, nx):
        start(("bias", d), bias.at[0], bias.at[nx - d], bias_s.at[d], bias_r.at[d], at(0, 0, d))

    for d in range(1, nx):
        start(("qdo", d), qdo.at[0], qdo.at[nx - d], qdo_s.at[d], qdo_r.at[d], at(0, 0, d))

    seam_send(1, query_ends)
    seam_over(0, window_ends)
    for d in range(1, nx):
        received("bias", d)
        received("qdo", d)
    queries = qdo[:, 0].reshape(nx * BLK, HD)
    grads = qdo[:, 1].reshape(nx * BLK, HD)
    half = ny * ROWS

    def strided(plane):
        for d in range(1, ny):
            received("y", plane, d)
        rows = pl.ds(plane * half, half)
        keys = kvg[plane, :, 0].reshape(half, HD)
        values = kvg[plane, :, 1].reshape(half, HD)
        s_ref[rows, :] = nt(keys, queries)
        dw_ref[rows, :] = nt(values, grads)

    strided(0)

    received("z", 0)
    for d in range(1, ny):
        start(("y", 1, d), kvg.at[1, 0], kvg.at[1, ny - d], y_s.at[1, d], y_r.at[1, d], at(0, d, 0))


    def columns(e, d):
        return pl.ds(pl.multiple_of(((g + e) % groups * group + (r + d) % group) * HD, HD), HD)

    w_loads = []
    for e in range(groups):
        to = pl.ds(e * HD, HD)
        load = pltpu.make_async_copy(w_hbm.at[:, columns(e, 0)], wg.at[0, :, to], w_local_sem.at[e])
        load.start()
        w_loads.append(load)
        for d in range(1, group):
            start(("w", d, e), w_hbm.at[:, columns(e, d)], wg.at[group - d, :, to], w_s.at[d, e], w_r.at[d, e], member(d))

    seam_land(0, window_ends)
    seam_received(0, window_ends)
    key_w = win[:, 0].reshape(3 * BLK, HD)
    value_w = win[:, 1].reshape(3 * BLK, HD)
    query_own, grad_own = qdo[0, 0], qdo[0, 1]
    score_w = nt(key_w, query_own) * SCALE
    top_w = jnp.max(score_w, axis=0, keepdims=True)
    p_w = jnp.exp(score_w - top_w)
    sum_w = jnp.sum(p_w, axis=0, keepdims=True)
    dw_w = nt(value_w, grad_own)
    delta_w = jnp.sum(p_w * dw_w, axis=0, keepdims=True)
    o_w = tn(value_w, p_w.astype(BF16))

    seam_over(1, query_ends)
    strided(1)
    chunks = nz * ny
    keys = kvg[:, :, 0].reshape(chunks * ROWS, HD)
    values = kvg[:, :, 1].reshape(chunks * ROWS, HD)
    tops, sums, deltas = [], [], []
    for i in range(nx):
        lanes = pl.ds(i * BLK, BLK)
        spread = jnp.broadcast_to(bias[i][:, None, :], (chunks, ROWS, BLK)).reshape(chunks * ROWS, BLK)
        score = s_ref[:, lanes] * SCALE + spread
        top = jnp.max(score, axis=0, keepdims=True)
        p = jnp.exp(score - top)
        s_ref[:, lanes] = p
        tops.append(top)
        sums.append(jnp.sum(p, axis=0, keepdims=True))
        deltas.append(jnp.sum(p * dw_ref[:, lanes], axis=0, keepdims=True))
    for i in range(nx):
        top, total, delta = tops[i], sums[i], deltas[i]
        if i == 0:
            top = jnp.maximum(tops[0], top_w)
            a, b = jnp.exp(tops[0] - top), jnp.exp(top_w - top)
            total = a * sums[0] + b * sum_w
            delta = a * deltas[0] + b * delta_w
        stats[0, i, 0:1, :] = top
        stats[0, i, 1:2, :] = total
        stats[0, i, 2:3, :] = delta
        stats[0, i, 3:8, :] = jnp.zeros((5, BLK), F32)
    for d in range(1, nx):
        start(("st", d), stats.at[0], stats.at[nx - d], st_s.at[d], st_r.at[d], at(0, 0, d))
    o_part = tn(values, s_ref[...].astype(BF16))
    for d in range(1, nx):
        osend[d] = o_part[:, d * BLK:(d + 1) * BLK].astype(BF16)
        start(("o", d), osend.at[d], orecv.at[nx - d], o_s.at[d], o_r.at[d], at(0, 0, d))
    for d in range(1, nx):
        received("st", d)

    logsums, all_deltas = [], []
    for i in range(nx):
        entries = [(stats[p, (i - p) % nx, 0:1, :], stats[p, (i - p) % nx, 1:2, :], stats[p, (i - p) % nx, 2:3, :]) for p in range(nx)]
        top = functools.reduce(jnp.maximum, [e[0] for e in entries])
        logsum = top + jnp.log(sum(e[1] * jnp.exp(e[0] - top) for e in entries))
        logsums.append(logsum)
        all_deltas.append(sum(e[2] * jnp.exp(e[0] - logsum) for e in entries))

    own_rows[0:1, :] = logsums[0]
    own_rows[1:2, :] = all_deltas[0]
    own_rows[2:8, :] = jnp.zeros((6, BLK), F32)
    for way in range(2):
        either(way, lambda copy: copy.start())

    weights, grad_scores = [], []
    for i in range(nx):
        lanes = pl.ds(i * BLK, BLK)
        probability = s_ref[:, lanes] * jnp.exp(tops[i] - logsums[i])
        weights.append(probability.astype(BF16))
        grad_scores.append((probability * (dw_ref[:, lanes] - all_deltas[i]) * SCALE).astype(BF16))
    weights = jnp.concatenate(weights, axis=1)
    grad_scores = jnp.concatenate(grad_scores, axis=1)
    gs[:, :, 0] = nn(grad_scores, queries).astype(BF16).reshape(nz, ny, ROWS, HD)
    gs[:, :, 1] = nn(weights, grads).astype(BF16).reshape(nz, ny, ROWS, HD)
    for d in range(1, ny):
        start(("gy", 1, d), gs.at[1, d], gy.at[1, ny - d], gy_s.at[1, d], gy_r.at[1, d], at(0, d, 0))

    factor_w = jnp.exp(top_w - logsums[0])
    prob_w = p_w * factor_w
    ds_w = (prob_w * (dw_w - all_deltas[0]) * SCALE).astype(BF16)
    own_k = nn(ds_w[BLK:2 * BLK], query_own)
    own_v = nn(prob_w[BLK:2 * BLK].astype(BF16), grad_own)

    attention = o_part[:, :BLK] * jnp.exp(tops[0] - logsums[0]) + o_w * factor_w
    for d in range(1, nx):
        p = nx - d
        received("o", d)
        attention = attention + orecv[p].astype(F32) * jnp.exp(stats[p, (-p) % nx, 0:1, :] - logsums[0])
    attg[0] = attention.astype(BF16)
    for d in range(1, group):
        start(("att", d), attg.at[0], attg.at[group - d], att_s.at[d], att_r.at[d], member(d))

    for way in range(2):
        @pl.when(ways[1 - way][0])
        def _():
            row_copy(way, True).wait_recv()
            row_relay(way).start()

    for d in range(1, ny):
        start(("gy", 0, d), gs.at[0, d], gy.at[0, ny - d], gy_s.at[0, d], gy_r.at[0, d], at(0, d, 0))

    seam_land(1, query_ends)

    dq = tn(keys, grad_scores)
    for d in range(1, nx):
        dqs[d] = dq[:, d * BLK:(d + 1) * BLK].astype(BF16)
        start(("dq", d), dqs.at[d], dqr.at[nx - d], dq_s.at[d], dq_r.at[d], at(0, 0, d))
    dq_own = dq[:, :BLK] + tn(key_w, ds_w)

    for load in w_loads:
        load.wait()
    for d in range(1, group):
        for e in range(groups):
            received("w", d, e)
        received("att", d)
    mixed = tn(attg[...].reshape(group * HD, BLK), wg[...].reshape(group * HD, groups * HD))
    for e in range(1, groups):
        msend[e] = mixed[:, e * HD:(e + 1) * HD].astype(BF16)
        start(("mix", e), msend.at[e], mrecv.at[groups - e], mix_s.at[e], mix_r.at[e], other_group(e))
    mixed_own = mixed[:, :HD]

    total = gs[1, 0].astype(F32)
    for d in range(1, ny):
        received("gy", 1, d)
        total = total + gy[1, ny - d].astype(F32)
    gzs[...] = total.astype(BF16)
    start(("gz", 0), gzs, gzr, gz_s.at[0], gz_r.at[0], at(1, 0, 0))

    for d in range(1, nx):
        received("dq", d)
        dq_own = dq_own + dqr[nx - d].astype(F32)
    out_ref[1] = dq_own.T.astype(BF16)

    seam_received(1, query_ends)
    for way in range(2):
        query_near, grad_near = near[way, 0], near[way, 1]
        score = nt(win[1, 0], query_near) * SCALE
        dw = nt(win[1, 1], grad_near)
        row_copy(way, False).wait_recv()
        probability = jnp.exp(score - near_rows[way, 0:1, :])
        ds = (probability * (dw - near_rows[way, 1:2, :]) * SCALE).astype(BF16)
        own_k = own_k + nn(ds, query_near)
        own_v = own_v + nn(probability.astype(BF16), grad_near)
    out_ref[2, ROWS:, :] = own_k[ROWS:].astype(BF16)
    out_ref[3, ROWS:, :] = own_v[ROWS:].astype(BF16)

    total = gs[0, 0].astype(F32)
    for d in range(1, ny):
        received("gy", 0, d)
        total = total + gy[0, ny - d].astype(F32)

    for e in range(1, groups):
        received("mix", e)
        mixed_own = mixed_own + mrecv[groups - e].astype(F32)
    out_ref[0] = mixed_own.astype(BF16)

    received("gz", 0)
    total = total + gzr[...].astype(F32)
    out_ref[2, :ROWS, :] = (own_k[:ROWS] + total[0]).astype(BF16)
    out_ref[3, :ROWS, :] = (own_v[:ROWS] + total[1]).astype(BF16)

    for copy in started.values():
        copy.wait_send()
    seam_sent(0, window_ends)
    seam_sent(1, query_ends)
    for way in range(2):
        either(way, lambda copy: copy.wait_send())

        @pl.when(ways[1 - way][0])
        def _():
            row_relay(way).wait_send()


def build(mesh, dims, group):
    nz, ny, nx = dims
    heads = mesh.shape["head"]
    groups = heads // group
    chunks = nz * ny

    def shards(queries, key_rows, value_rows, out_weight, strided_index, cotangent):
        width = out_weight.shape[1]
        dma = pltpu.SemaphoreType.DMA
        hbm = pl.BlockSpec(memory_space=pl.ANY)
        vmem = pl.BlockSpec(memory_space=pltpu.VMEM)
        square = lambda n: pltpu.VMEM((n, BLK, HD), BF16)
        pieces = lambda: pltpu.VMEM((nz, ny, 2, ROWS, HD), BF16)
        out = pl.pallas_call(
            functools.partial(kernel, dims, group, heads),
            out_shape=jax.ShapeDtypeStruct((4, BLK, HD), BF16),
            in_specs=[hbm, hbm, hbm, hbm, pl.BlockSpec(memory_space=pltpu.SMEM), hbm],
            out_specs=vmem,
            scratch_shapes=[
                pltpu.VMEM((HD, width), BF16),
                pltpu.VMEM((BLK, width), BF16),
                pltpu.VMEM((3, 2, BLK, HD), BF16),
                pieces(),
                pltpu.VMEM((nx, 2, BLK, HD), BF16),
                pltpu.VMEM((nx, chunks, BLK), F32),
                pltpu.VMEM((group, HD, groups * HD), BF16),
                pltpu.VMEM((nx, nx, 8, BLK), F32),
                square(nx), square(nx),
                square(group),
                square(groups), square(groups),
                square(nx), square(nx),
                pltpu.VMEM((2, 2, BLK, HD), BF16), pltpu.VMEM((8, BLK), F32), pltpu.VMEM((2, 8, BLK), F32), pltpu.VMEM((2, 8, BLK), F32),
                pieces(), pieces(),
                pltpu.VMEM((2, ROWS, HD), BF16), pltpu.VMEM((2, ROWS, HD), BF16),
                pltpu.VMEM((chunks * ROWS, nx * BLK), F32),
                pltpu.VMEM((chunks * ROWS, nx * BLK), F32),
                pltpu.VMEM((2, 2, 2, BLK // 4, HD), BF16), pltpu.VMEM((2, 2, 2, BLK // 4, HD), BF16),
                dma((5,)), dma((groups,)),
                dma((1,)), dma((1,)),
                dma((2, ny)), dma((2, ny)),
                dma((2, 2)), dma((2, 2)),
                dma((2, 2, 4)), dma((2, 2)), dma((2, 2)), dma((2, 2)), dma((2, 2)),
                dma((2,)), dma((2,)), dma((2,)), dma((2,)),
                dma((nx,)), dma((nx,)),
                dma((nx,)), dma((nx,)),
                dma((group, groups)), dma((group, groups)),
                dma((nx,)), dma((nx,)),
                dma((nx,)), dma((nx,)),
                dma((nx,)), dma((nx,)),
                dma((2, ny)), dma((2, ny)),
                dma((1,)), dma((1,)),
                dma((group,)), dma((group,)),
                dma((groups,)), dma((groups,)),
            ],
            compiler_params=pltpu.CompilerParams(
                collective_id=0, has_side_effects=True, vmem_limit_bytes=56 * 2 ** 20
            ),
        )(queries, key_rows, value_rows, out_weight, strided_index, cotangent)
        return tuple(out[i] for i in range(4))

    spread = P("seq", "head")
    return jax.shard_map(
        shards,
        mesh=mesh,
        in_specs=(spread, spread, spread, P("head", None), P("seq", None), P("seq", None)),
        out_specs=(spread,) * 4,
        check_vma=False,
    )


def solution(mesh):
    return build(mesh, GRID, GROUP)
```

```python
import functools

import jax
import jax.numpy as jnp
from jax import lax
from jax.experimental import pallas as pl
from jax.experimental.pallas import tpu as pltpu
from jax.sharding import PartitionSpec as P

HD = 128
BLK = 128
ROWS = 32
GRID = (2, 8, 4)
GROUP = 4
MESH = pl.DeviceIdType.MESH
F32 = jnp.float32
BF16 = jnp.bfloat16
SCALE = HD ** -0.5
EXCLUDED = -1e30


def nt(a, b):
    return lax.dot_general(a, b, (((1,), (1,)), ((), ())), preferred_element_type=F32)


def nn(a, b):
    return lax.dot_general(a, b, (((1,), (0,)), ((), ())), preferred_element_type=F32)


def tn(a, b):
    return lax.dot_general(a, b, (((0,), (0,)), ((), ())), preferred_element_type=F32)


def kernel(
    dims, group, heads,
    q_hbm, k_hbm, v_hbm, w_hbm, index_ref, ct_hbm,
    out_ref,
    w_ref, ct_ref, win, kvg, qdo, bias, wg, stats, osend, orecv, attg, msend, mrecv,
    dqs, dqr, near, own_rows, near_rows, relay_rows, gs, gy, gzs, gzr, s_ref, dw_ref, seam_a, seam_b,
    local_sem, w_local_sem,
    z_s, z_r, y_s, y_r, win_s, win_r, out_s, in_r, over_s, over_r, last_s, row_s, row_r, relay_s, relay_r, qdo_s, qdo_r, bias_s, bias_r, w_s, w_r,
    st_s, st_r, o_s, o_r, dq_s, dq_r, gy_s, gy_r, gz_s, gz_r, att_s, att_r, mix_s, mix_r,
):
    nz, ny, nx = dims
    groups = heads // group
    seq = lax.axis_index("seq")
    head = lax.axis_index("head")
    z, y, x = seq // (ny * nx), (seq // nx) % ny, seq % nx
    g, r = head // group, head % group

    def at(dz, dy, dx):
        return (((z + dz) % nz * ny + (y + dy) % ny) * nx + (x + dx) % nx, head)

    def member(d):
        return (seq, g * group + (r + d) % group)

    def other_group(e):
        return (seq, (g + e) % groups * group + r)

    plane = ny * nx
    place = seq % plane
    following = (z * plane + (place + 1) % plane, head)
    preceding = (z * plane + (place + plane - 1) % plane, head)

    def send(src, dst, send_sem, recv_sem, device):
        return pltpu.make_async_remote_copy(
            src_ref=src, dst_ref=dst, send_sem=send_sem, recv_sem=recv_sem,
            device_id=device, device_id_type=MESH,
        )

    started, waited = {}, set()

    def start(name, src, dst, send_sem, recv_sem, device):
        copy = send(src, dst, send_sem, recv_sem, device)
        copy.start()
        started[name] = copy

    def received(*name):
        started[name].wait_recv()
        waited.add(name)

    pieces, piece = 4, BLK // 4
    is_last = (y == ny - 1) & (x == nx - 1)
    is_first = (y == 0) & (x == 0)
    corner = ((y == 0) | (y == ny - 1)) & ((x == 0) | (x == nx - 1))
    low = (y == 0).astype(jnp.int32) + 2 * (x == 0).astype(jnp.int32)
    ways = (
        (is_last, 1, following, low, at(0, -y, -x)),
        (is_first, -1, preceding, 3 - low, at(0, ny - 1 - y, nx - 1 - x)),
    )

    def whole(kind, way, src, dst):
        return send(src, dst, win_s.at[kind, way], win_r.at[kind, way], ways[way][2])

    def scattered(kind, way, src):
        step = ways[way][1]
        return [
            send(src.at[:, t * piece:(t + 1) * piece], seam_a.at[kind, way], out_s.at[kind, way, t], in_r.at[kind, way], at(0, step * (t & 1), step * (t >> 1)))
            for t in range(1, pieces)
        ]

    def over(kind, way):
        return send(seam_a.at[kind, way], seam_b.at[kind, way], over_s.at[kind, way], over_r.at[kind, way], at(1, 0, 0))

    def over_last(kind, way, dst):
        return send(seam_a.at[kind, way], dst.at[:, (pieces - 1) * piece:], over_s.at[kind, way], win_r.at[kind, way], at(1, 0, 0))

    def landing(kind, way, dst):
        rows = pl.ds(pl.multiple_of(ways[way][3] * piece, piece), piece)
        return send(seam_b.at[kind, way], dst.at[:, rows], last_s.at[kind, way], win_r.at[kind, way], ways[way][4])

    def outer(kind, way):
        return (x == (0 if way else nx - 1)) | (kind == 0)

    def seam_send(kind, ends):
        for way, (src, dst) in enumerate(ends):
            source = ways[way][0]
            outside = outer(kind, way)

            @pl.when(source)
            def _():
                for copy in scattered(kind, way, src):
                    copy.start()
                seam_a[kind, way] = src[:, :piece]

            @pl.when(jnp.logical_not(source) & outside)
            def _():
                whole(kind, way, src, dst).start()

    def seam_over(kind, ends):
        for way, (src, dst) in enumerate(ends):
            number = ways[way][3]

            @pl.when(corner & (number > 0))
            def _():
                scattered(kind, way, src)[0].wait_recv()

            @pl.when(corner & (number < pieces - 1))
            def _():
                over(kind, way).start()

            @pl.when(corner & (number == pieces - 1))
            def _():
                over_last(kind, way, dst).start()

    def seam_land(kind, ends):
        for way, (src, dst) in enumerate(ends):
            @pl.when(corner & (ways[way][3] < pieces - 1))
            def _():
                over(kind, way).wait_recv()
                landing(kind, way, dst).start()

    def seam_received(kind, ends):
        for way, (src, dst) in enumerate(ends):
            outside = outer(kind, 1 - way)

            @pl.when(outside)
            def _():
                whole(kind, way, src, dst).wait_recv()

            if kind == 1:
                @pl.when(jnp.logical_not(outside))
                def _():
                    dst[...] = qdo[1 if way else nx - 1]

    def seam_sent(kind, ends):
        for way, (src, dst) in enumerate(ends):
            source, number = ways[way][0], ways[way][3]

            @pl.when(source)
            def _():
                for copy in scattered(kind, way, src):
                    copy.wait_send()

            @pl.when(jnp.logical_not(source) & outer(kind, way))
            def _():
                whole(kind, way, src, dst).wait_send()

            @pl.when(corner)
            def _():
                over(kind, way).wait_send()

            @pl.when(corner & (number < pieces - 1))
            def _():
                landing(kind, way, dst).wait_send()

    def row_copy(way, source):
        to, arrived = (relay_rows.at[way], relay_r.at[way]) if source else (near_rows.at[way], row_r.at[way])
        return send(own_rows, to, row_s.at[way], arrived, ways[way][2])

    def row_relay(way):
        return send(relay_rows.at[way], near_rows.at[way], relay_s.at[way], row_r.at[way], at(1, 0, 0))

    def either(way, action):
        for source in (True, False):
            @pl.when(ways[way][0] == source)
            def _():
                action(row_copy(way, source))

    window_ends = ((win.at[1], win.at[0]), (win.at[1], win.at[2]))
    query_ends = ((qdo.at[0], near.at[0]), (qdo.at[0], near.at[1]))

    partners = [at(1, 0, 0)]
    partners += [at(0, d, 0) for d in range(1, ny)]
    partners += [at(0, 0, d) for d in range(1, nx)]
    partners += [following, preceding]
    partners += [member(d) for d in range(1, group)]
    partners += [other_group(e) for e in range(1, groups)]
    barrier = pltpu.get_barrier_semaphore()

    for device in partners:
        pl.semaphore_signal(barrier, inc=1, device_id=device, device_id_type=MESH)

    loads = [
        pltpu.make_async_copy(k_hbm, win.at[1, 0], local_sem.at[0]),
        pltpu.make_async_copy(v_hbm, win.at[1, 1], local_sem.at[1]),
        pltpu.make_async_copy(q_hbm, qdo.at[0, 0], local_sem.at[2]),
        pltpu.make_async_copy(w_hbm, w_ref, local_sem.at[3]),
        pltpu.make_async_copy(ct_hbm, ct_ref, local_sem.at[4]),
    ]
    for load in loads:
        load.start()

    row = lax.broadcasted_iota(jnp.int32, (nz * ny, BLK), 0)
    block = ((z + row // ny) % nz * ny + (y + row % ny) % ny) * nx // (BLK // ROWS)
    listed = jnp.zeros((nz * ny, BLK), F32)
    for slot in range(index_ref.shape[1]):
        listed = listed + (block == index_ref[0, slot]).astype(F32)
    bias[0] = jnp.where(listed > 0, jnp.log(jnp.maximum(listed, 1.0)), EXCLUDED)

    loads[0].wait()
    loads[1].wait()
    kvg[0, 0] = win[1, :, :ROWS, :]
    loads[2].wait()
    loads[3].wait()
    loads[4].wait()
    qdo[0, 1] = nt(ct_ref[...], w_ref[...]).astype(BF16)
    pl.semaphore_wait(barrier, len(partners))

    start(("z", 0), kvg.at[0, 0], kvg.at[1, 0], z_s.at[0], z_r.at[0], at(1, 0, 0))
    seam_send(0, window_ends)
    for d in range(1, ny):
        start(("y", 0, d), kvg.at[0, 0], kvg.at[0, ny - d], y_s.at[0, d], y_r.at[0, d], at(0, d, 0))
    for d in range(1, nx):
        start(("bias", d), bias.at[0], bias.at[nx - d], bias_s.at[d], bias_r.at[d], at(0, 0, d))

    for d in range(1, nx):
        start(("qdo", d), qdo.at[0], qdo.at[nx - d], qdo_s.at[d], qdo_r.at[d], at(0, 0, d))

    seam_over(0, window_ends)
    received("z", 0)
    for d in range(1, ny):
        start(("y", 1, d), kvg.at[1, 0], kvg.at[1, ny - d], y_s.at[1, d], y_r.at[1, d], at(0, d, 0))


    seam_send(1, query_ends)
    for d in range(1, nx):
        received("bias", d)
        received("qdo", d)
    queries = qdo[:, 0].reshape(nx * BLK, HD)
    grads = qdo[:, 1].reshape(nx * BLK, HD)
    half = ny * ROWS

    def strided(plane):
        for d in range(1, ny):
            received("y", plane, d)
        rows = pl.ds(plane * half, half)
        keys = kvg[plane, :, 0].reshape(half, HD)
        values = kvg[plane, :, 1].reshape(half, HD)
        s_ref[rows, :] = nt(keys, queries)
        dw_ref[rows, :] = nt(values, grads)

    strided(0)

    def columns(e, d):
        return pl.ds(pl.multiple_of(((g + e) % groups * group + (r + d) % group) * HD, HD), HD)

    w_loads = []
    for e in range(groups):
        to = pl.ds(e * HD, HD)
        load = pltpu.make_async_copy(w_hbm.at[:, columns(e, 0)], wg.at[0, :, to], w_local_sem.at[e])
        load.start()
        w_loads.append(load)
        for d in range(1, group):
            start(("w", d, e), w_hbm.at[:, columns(e, d)], wg.at[group - d, :, to], w_s.at[d, e], w_r.at[d, e], member(d))

    seam_land(0, window_ends)
    seam_received(0, window_ends)
    key_w = win[:, 0].reshape(3 * BLK, HD)
    value_w = win[:, 1].reshape(3 * BLK, HD)
    query_own, grad_own = qdo[0, 0], qdo[0, 1]
    score_w = nt(key_w, query_own) * SCALE
    top_w = jnp.max(score_w, axis=0, keepdims=True)
    p_w = jnp.exp(score_w - top_w)
    sum_w = jnp.sum(p_w, axis=0, keepdims=True)
    dw_w = nt(value_w, grad_own)
    delta_w = jnp.sum(p_w * dw_w, axis=0, keepdims=True)
    o_w = tn(value_w, p_w.astype(BF16))

    seam_over(1, query_ends)
    strided(1)
    chunks = nz * ny
    keys = kvg[:, :, 0].reshape(chunks * ROWS, HD)
    values = kvg[:, :, 1].reshape(chunks * ROWS, HD)
    tops, sums, deltas = [], [], []
    for i in range(nx):
        lanes = pl.ds(i * BLK, BLK)
        spread = jnp.broadcast_to(bias[i][:, None, :], (chunks, ROWS, BLK)).reshape(chunks * ROWS, BLK)
        score = s_ref[:, lanes] * SCALE + spread
        top = jnp.max(score, axis=0, keepdims=True)
        p = jnp.exp(score - top)
        s_ref[:, lanes] = p
        tops.append(top)
        sums.append(jnp.sum(p, axis=0, keepdims=True))
        deltas.append(jnp.sum(p * dw_ref[:, lanes], axis=0, keepdims=True))
    for i in range(nx):
        top, total, delta = tops[i], sums[i], deltas[i]
        if i == 0:
            top = jnp.maximum(tops[0], top_w)
            a, b = jnp.exp(tops[0] - top), jnp.exp(top_w - top)
            total = a * sums[0] + b * sum_w
            delta = a * deltas[0] + b * delta_w
        stats[0, i, 0:1, :] = top
        stats[0, i, 1:2, :] = total
        stats[0, i, 2:3, :] = delta
        stats[0, i, 3:8, :] = jnp.zeros((5, BLK), F32)
    for d in range(1, nx):
        start(("st", d), stats.at[0], stats.at[nx - d], st_s.at[d], st_r.at[d], at(0, 0, d))
    o_part = tn(values, s_ref[...].astype(BF16))
    for d in range(1, nx):
        osend[d] = o_part[:, d * BLK:(d + 1) * BLK].astype(BF16)
        start(("o", d), osend.at[d], orecv.at[nx - d], o_s.at[d], o_r.at[d], at(0, 0, d))
    for d in range(1, nx):
        received("st", d)

    logsums, all_deltas = [], []
    for i in range(nx):
        entries = [(stats[p, (i - p) % nx, 0:1, :], stats[p, (i - p) % nx, 1:2, :], stats[p, (i - p) % nx, 2:3, :]) for p in range(nx)]
        top = functools.reduce(jnp.maximum, [e[0] for e in entries])
        logsum = top + jnp.log(sum(e[1] * jnp.exp(e[0] - top) for e in entries))
        logsums.append(logsum)
        all_deltas.append(sum(e[2] * jnp.exp(e[0] - logsum) for e in entries))

    own_rows[0:1, :] = logsums[0]
    own_rows[1:2, :] = all_deltas[0]
    own_rows[2:8, :] = jnp.zeros((6, BLK), F32)
    for way in range(2):
        either(way, lambda copy: copy.start())

    weights, grad_scores = [], []
    for i in range(nx):
        lanes = pl.ds(i * BLK, BLK)
        probability = s_ref[:, lanes] * jnp.exp(tops[i] - logsums[i])
        weights.append(probability.astype(BF16))
        grad_scores.append((probability * (dw_ref[:, lanes] - all_deltas[i]) * SCALE).astype(BF16))
    weights = jnp.concatenate(weights, axis=1)
    grad_scores = jnp.concatenate(grad_scores, axis=1)
    def collect(plane):
        rows = slice(plane * half, (plane + 1) * half)
        gs[plane, :, 0] = nn(grad_scores[rows], queries).astype(BF16).reshape(ny, ROWS, HD)
        gs[plane, :, 1] = nn(weights[rows], grads).astype(BF16).reshape(ny, ROWS, HD)

    collect(1)
    for d in range(1, ny):
        start(("gy", 1, d), gs.at[1, d], gy.at[1, ny - d], gy_s.at[1, d], gy_r.at[1, d], at(0, d, 0))

    factor_w = jnp.exp(top_w - logsums[0])
    prob_w = p_w * factor_w
    ds_w = (prob_w * (dw_w - all_deltas[0]) * SCALE).astype(BF16)
    own_k = nn(ds_w[BLK:2 * BLK], query_own)
    own_v = nn(prob_w[BLK:2 * BLK].astype(BF16), grad_own)

    attention = o_part[:, :BLK] * jnp.exp(tops[0] - logsums[0]) + o_w * factor_w
    for d in range(1, nx):
        p = nx - d
        received("o", d)
        attention = attention + orecv[p].astype(F32) * jnp.exp(stats[p, (-p) % nx, 0:1, :] - logsums[0])
    attg[0] = attention.astype(BF16)
    for d in range(1, group):
        start(("att", d), attg.at[0], attg.at[group - d], att_s.at[d], att_r.at[d], member(d))

    for way in range(2):
        @pl.when(ways[1 - way][0])
        def _():
            row_copy(way, True).wait_recv()
            row_relay(way).start()

    collect(0)
    for d in range(1, ny):
        start(("gy", 0, d), gs.at[0, d], gy.at[0, ny - d], gy_s.at[0, d], gy_r.at[0, d], at(0, d, 0))

    seam_land(1, query_ends)

    dq = tn(keys, grad_scores)
    for d in range(1, nx):
        dqs[d] = dq[:, d * BLK:(d + 1) * BLK].astype(BF16)
        start(("dq", d), dqs.at[d], dqr.at[nx - d], dq_s.at[d], dq_r.at[d], at(0, 0, d))
    dq_own = dq[:, :BLK] + tn(key_w, ds_w)

    for load in w_loads:
        load.wait()
    for d in range(1, group):
        for e in range(groups):
            received("w", d, e)
        received("att", d)
    mixed = tn(attg[...].reshape(group * HD, BLK), wg[...].reshape(group * HD, groups * HD))
    for e in range(1, groups):
        msend[e] = mixed[:, e * HD:(e + 1) * HD].astype(BF16)
        start(("mix", e), msend.at[e], mrecv.at[groups - e], mix_s.at[e], mix_r.at[e], other_group(e))
    mixed_own = mixed[:, :HD]

    total = gs[1, 0].astype(F32)
    for d in range(1, ny):
        received("gy", 1, d)
        total = total + gy[1, ny - d].astype(F32)
    gzs[...] = total.astype(BF16)
    start(("gz", 0), gzs, gzr, gz_s.at[0], gz_r.at[0], at(1, 0, 0))

    for d in range(1, nx):
        received("dq", d)
        dq_own = dq_own + dqr[nx - d].astype(F32)
    out_ref[1] = dq_own.T.astype(BF16)

    seam_received(1, query_ends)
    for way in range(2):
        query_near, grad_near = near[way, 0], near[way, 1]
        score = nt(win[1, 0], query_near) * SCALE
        dw = nt(win[1, 1], grad_near)
        row_copy(way, False).wait_recv()
        probability = jnp.exp(score - near_rows[way, 0:1, :])
        ds = (probability * (dw - near_rows[way, 1:2, :]) * SCALE).astype(BF16)
        own_k = own_k + nn(ds, query_near)
        own_v = own_v + nn(probability.astype(BF16), grad_near)
    out_ref[2, ROWS:, :] = own_k[ROWS:].astype(BF16)
    out_ref[3, ROWS:, :] = own_v[ROWS:].astype(BF16)

    total = gs[0, 0].astype(F32)
    for d in range(1, ny):
        received("gy", 0, d)
        total = total + gy[0, ny - d].astype(F32)

    for e in range(1, groups):
        received("mix", e)
        mixed_own = mixed_own + mrecv[groups - e].astype(F32)
    out_ref[0] = mixed_own.astype(BF16)

    received("gz", 0)
    total = total + gzr[...].astype(F32)
    out_ref[2, :ROWS, :] = (own_k[:ROWS] + total[0]).astype(BF16)
    out_ref[3, :ROWS, :] = (own_v[:ROWS] + total[1]).astype(BF16)

    for copy in started.values():
        copy.wait_send()
    seam_sent(0, window_ends)
    seam_sent(1, query_ends)
    for way in range(2):
        either(way, lambda copy: copy.wait_send())

        @pl.when(ways[1 - way][0])
        def _():
            row_relay(way).wait_send()


def build(mesh, dims, group):
    nz, ny, nx = dims
    heads = mesh.shape["head"]
    groups = heads // group
    chunks = nz * ny

    def shards(queries, key_rows, value_rows, out_weight, strided_index, cotangent):
        width = out_weight.shape[1]
        dma = pltpu.SemaphoreType.DMA
        hbm = pl.BlockSpec(memory_space=pl.ANY)
        vmem = pl.BlockSpec(memory_space=pltpu.VMEM)
        square = lambda n: pltpu.VMEM((n, BLK, HD), BF16)
        pieces = lambda: pltpu.VMEM((nz, ny, 2, ROWS, HD), BF16)
        out = pl.pallas_call(
            functools.partial(kernel, dims, group, heads),
            out_shape=jax.ShapeDtypeStruct((4, BLK, HD), BF16),
            in_specs=[hbm, hbm, hbm, hbm, pl.BlockSpec(memory_space=pltpu.SMEM), hbm],
            out_specs=vmem,
            scratch_shapes=[
                pltpu.VMEM((HD, width), BF16),
                pltpu.VMEM((BLK, width), BF16),
                pltpu.VMEM((3, 2, BLK, HD), BF16),
                pieces(),
                pltpu.VMEM((nx, 2, BLK, HD), BF16),
                pltpu.VMEM((nx, chunks, BLK), F32),
                pltpu.VMEM((group, HD, groups * HD), BF16),
                pltpu.VMEM((nx, nx, 8, BLK), F32),
                square(nx), square(nx),
                square(group),
                square(groups), square(groups),
                square(nx), square(nx),
                pltpu.VMEM((2, 2, BLK, HD), BF16), pltpu.VMEM((8, BLK), F32), pltpu.VMEM((2, 8, BLK), F32), pltpu.VMEM((2, 8, BLK), F32),
                pieces(), pieces(),
                pltpu.VMEM((2, ROWS, HD), BF16), pltpu.VMEM((2, ROWS, HD), BF16),
                pltpu.VMEM((chunks * ROWS, nx * BLK), F32),
                pltpu.VMEM((chunks * ROWS, nx * BLK), F32),
                pltpu.VMEM((2, 2, 2, BLK // 4, HD), BF16), pltpu.VMEM((2, 2, 2, BLK // 4, HD), BF16),
                dma((5,)), dma((groups,)),
                dma((1,)), dma((1,)),
                dma((2, ny)), dma((2, ny)),
                dma((2, 2)), dma((2, 2)),
                dma((2, 2, 4)), dma((2, 2)), dma((2, 2)), dma((2, 2)), dma((2, 2)),
                dma((2,)), dma((2,)), dma((2,)), dma((2,)),
                dma((nx,)), dma((nx,)),
                dma((nx,)), dma((nx,)),
                dma((group, groups)), dma((group, groups)),
                dma((nx,)), dma((nx,)),
                dma((nx,)), dma((nx,)),
                dma((nx,)), dma((nx,)),
                dma((2, ny)), dma((2, ny)),
                dma((1,)), dma((1,)),
                dma((group,)), dma((group,)),
                dma((groups,)), dma((groups,)),
            ],
            compiler_params=pltpu.CompilerParams(
                collective_id=0, has_side_effects=True, vmem_limit_bytes=56 * 2 ** 20
            ),
        )(queries, key_rows, value_rows, out_weight, strided_index, cotangent)
        return tuple(out[i] for i in range(4))

    spread = P("seq", "head")
    return jax.shard_map(
        shards,
        mesh=mesh,
        in_specs=(spread, spread, spread, P("head", None), P("seq", None), P("seq", None)),
        out_specs=(spread,) * 4,
        check_vma=False,
    )


def solution(mesh):
    return build(mesh, GRID, GROUP)
```

```python
import functools

import jax
import jax.numpy as jnp
from jax import lax
from jax.experimental import pallas as pl
from jax.experimental.pallas import tpu as pltpu
from jax.sharding import PartitionSpec as P

HD = 128
BLK = 128
ROWS = 32
GRID = (2, 8, 4)
GROUP = 4
MESH = pl.DeviceIdType.MESH
F32 = jnp.float32
BF16 = jnp.bfloat16
SCALE = HD ** -0.5
EXCLUDED = -1e30


def far(size):
    return sorted(range(1, size), key=lambda d: -min(d, size - d))


def nt(a, b):
    return lax.dot_general(a, b, (((1,), (1,)), ((), ())), preferred_element_type=F32)


def nn(a, b):
    return lax.dot_general(a, b, (((1,), (0,)), ((), ())), preferred_element_type=F32)


def tn(a, b):
    return lax.dot_general(a, b, (((0,), (0,)), ((), ())), preferred_element_type=F32)


def kernel(
    dims, group, heads,
    q_hbm, k_hbm, v_hbm, w_hbm, index_ref, ct_hbm,
    out_ref,
    w_ref, ct_ref, win, kvg, qdo, bias, wg, stats, osend, orecv, attg, msend, mrecv,
    dqs, dqr, near, own_rows, near_rows, relay_rows, gs, gy, gzs, gzr, s_ref, dw_ref, seam_a, seam_b,
    local_sem, w_local_sem,
    z_s, z_r, y_s, y_r, win_s, win_r, out_s, in_r, over_s, over_r, last_s, row_s, row_r, relay_s, relay_r, qdo_s, qdo_r, bias_s, bias_r, w_s, w_r,
    st_s, st_r, o_s, o_r, dq_s, dq_r, gy_s, gy_r, gz_s, gz_r, att_s, att_r, mix_s, mix_r,
):
    nz, ny, nx = dims
    groups = heads // group
    seq = lax.axis_index("seq")
    head = lax.axis_index("head")
    z, y, x = seq // (ny * nx), (seq // nx) % ny, seq % nx
    g, r = head // group, head % group

    def at(dz, dy, dx):
        return (((z + dz) % nz * ny + (y + dy) % ny) * nx + (x + dx) % nx, head)

    def member(d):
        return (seq, g * group + (r + d) % group)

    def other_group(e):
        return (seq, (g + e) % groups * group + r)

    plane = ny * nx
    place = seq % plane
    following = (z * plane + (place + 1) % plane, head)
    preceding = (z * plane + (place + plane - 1) % plane, head)

    def send(src, dst, send_sem, recv_sem, device):
        return pltpu.make_async_remote_copy(
            src_ref=src, dst_ref=dst, send_sem=send_sem, recv_sem=recv_sem,
            device_id=device, device_id_type=MESH,
        )

    started, waited = {}, set()

    def start(name, src, dst, send_sem, recv_sem, device):
        copy = send(src, dst, send_sem, recv_sem, device)
        copy.start()
        started[name] = copy

    def received(*name):
        started[name].wait_recv()
        waited.add(name)

    pieces, piece = 4, BLK // 4
    is_last = (y == ny - 1) & (x == nx - 1)
    is_first = (y == 0) & (x == 0)
    corner = ((y == 0) | (y == ny - 1)) & ((x == 0) | (x == nx - 1))
    low = (y == 0).astype(jnp.int32) + 2 * (x == 0).astype(jnp.int32)
    ways = (
        (is_last, 1, following, low, at(0, -y, -x)),
        (is_first, -1, preceding, 3 - low, at(0, ny - 1 - y, nx - 1 - x)),
    )

    def whole(kind, way, src, dst):
        return send(src, dst, win_s.at[kind, way], win_r.at[kind, way], ways[way][2])

    def scattered(kind, way, src):
        step = ways[way][1]
        return [
            send(src.at[:, t * piece:(t + 1) * piece], seam_a.at[kind, way], out_s.at[kind, way, t], in_r.at[kind, way], at(0, step * (t & 1), step * (t >> 1)))
            for t in range(1, pieces)
        ]

    def over(kind, way):
        return send(seam_a.at[kind, way], seam_b.at[kind, way], over_s.at[kind, way], over_r.at[kind, way], at(1, 0, 0))

    def over_last(kind, way, dst):
        return send(seam_a.at[kind, way], dst.at[:, (pieces - 1) * piece:], over_s.at[kind, way], win_r.at[kind, way], at(1, 0, 0))

    def landing(kind, way, dst):
        rows = pl.ds(pl.multiple_of(ways[way][3] * piece, piece), piece)
        return send(seam_b.at[kind, way], dst.at[:, rows], last_s.at[kind, way], win_r.at[kind, way], ways[way][4])

    def outer(kind, way):
        return (x == (0 if way else nx - 1)) | (kind == 0)

    def seam_send(kind, ends):
        for way, (src, dst) in enumerate(ends):
            source = ways[way][0]
            outside = outer(kind, way)

            @pl.when(source)
            def _():
                for copy in scattered(kind, way, src):
                    copy.start()
                seam_a[kind, way] = src[:, :piece]

            @pl.when(jnp.logical_not(source) & outside)
            def _():
                whole(kind, way, src, dst).start()

    def seam_over(kind, ends):
        for way, (src, dst) in enumerate(ends):
            number = ways[way][3]

            @pl.when(corner & (number > 0))
            def _():
                scattered(kind, way, src)[0].wait_recv()

            @pl.when(corner & (number < pieces - 1))
            def _():
                over(kind, way).start()

            @pl.when(corner & (number == pieces - 1))
            def _():
                over_last(kind, way, dst).start()

    def seam_land(kind, ends):
        for way, (src, dst) in enumerate(ends):
            @pl.when(corner & (ways[way][3] < pieces - 1))
            def _():
                over(kind, way).wait_recv()
                landing(kind, way, dst).start()

    def seam_received(kind, ends):
        for way, (src, dst) in enumerate(ends):
            outside = outer(kind, 1 - way)

            @pl.when(outside)
            def _():
                whole(kind, way, src, dst).wait_recv()

            if kind == 1:
                @pl.when(jnp.logical_not(outside))
                def _():
                    dst[...] = qdo[1 if way else nx - 1]

    def seam_sent(kind, ends):
        for way, (src, dst) in enumerate(ends):
            source, number = ways[way][0], ways[way][3]

            @pl.when(source)
            def _():
                for copy in scattered(kind, way, src):
                    copy.wait_send()

            @pl.when(jnp.logical_not(source) & outer(kind, way))
            def _():
                whole(kind, way, src, dst).wait_send()

            @pl.when(corner)
            def _():
                over(kind, way).wait_send()

            @pl.when(corner & (number < pieces - 1))
            def _():
                landing(kind, way, dst).wait_send()

    def row_copy(way, source):
        to, arrived = (relay_rows.at[way], relay_r.at[way]) if source else (near_rows.at[way], row_r.at[way])
        return send(own_rows, to, row_s.at[way], arrived, ways[way][2])

    def row_relay(way):
        return send(relay_rows.at[way], near_rows.at[way], relay_s.at[way], row_r.at[way], at(1, 0, 0))

    def either(way, action):
        for source in (True, False):
            @pl.when(ways[way][0] == source)
            def _():
                action(row_copy(way, source))

    window_ends = ((win.at[1], win.at[0]), (win.at[1], win.at[2]))
    query_ends = ((qdo.at[0], near.at[0]), (qdo.at[0], near.at[1]))

    partners = [at(1, 0, 0)]
    partners += [at(0, d, 0) for d in range(1, ny)]
    partners += [at(0, 0, d) for d in range(1, nx)]
    partners += [following, preceding]
    partners += [member(d) for d in range(1, group)]
    partners += [other_group(e) for e in range(1, groups)]
    barrier = pltpu.get_barrier_semaphore()

    for device in partners:
        pl.semaphore_signal(barrier, inc=1, device_id=device, device_id_type=MESH)

    loads = [
        pltpu.make_async_copy(k_hbm, win.at[1, 0], local_sem.at[0]),
        pltpu.make_async_copy(v_hbm, win.at[1, 1], local_sem.at[1]),
        pltpu.make_async_copy(q_hbm, qdo.at[0, 0], local_sem.at[2]),
        pltpu.make_async_copy(w_hbm, w_ref, local_sem.at[3]),
        pltpu.make_async_copy(ct_hbm, ct_ref, local_sem.at[4]),
    ]
    for load in loads:
        load.start()

    row = lax.broadcasted_iota(jnp.int32, (nz * ny, BLK), 0)
    block = ((z + row // ny) % nz * ny + (y + row % ny) % ny) * nx // (BLK // ROWS)
    listed = jnp.zeros((nz * ny, BLK), F32)
    for slot in range(index_ref.shape[1]):
        listed = listed + (block == index_ref[0, slot]).astype(F32)
    bias[0] = jnp.where(listed > 0, jnp.log(jnp.maximum(listed, 1.0)), EXCLUDED)

    loads[0].wait()
    loads[1].wait()
    kvg[0, 0] = win[1, :, :ROWS, :]
    loads[2].wait()
    loads[3].wait()
    loads[4].wait()
    qdo[0, 1] = nt(ct_ref[...], w_ref[...]).astype(BF16)
    pl.semaphore_wait(barrier, len(partners))

    start(("z", 0), kvg.at[0, 0], kvg.at[1, 0], z_s.at[0], z_r.at[0], at(1, 0, 0))
    seam_send(0, window_ends)
    for d in far(ny):
        start(("y", 0, d), kvg.at[0, 0], kvg.at[0, ny - d], y_s.at[0, d], y_r.at[0, d], at(0, d, 0))
    for d in far(nx):
        start(("bias", d), bias.at[0], bias.at[nx - d], bias_s.at[d], bias_r.at[d], at(0, 0, d))

    for d in far(nx):
        start(("qdo", d), qdo.at[0], qdo.at[nx - d], qdo_s.at[d], qdo_r.at[d], at(0, 0, d))

    seam_over(0, window_ends)
    received("z", 0)
    for d in far(ny):
        start(("y", 1, d), kvg.at[1, 0], kvg.at[1, ny - d], y_s.at[1, d], y_r.at[1, d], at(0, d, 0))


    seam_send(1, query_ends)
    for d in range(1, nx):
        received("bias", d)
        received("qdo", d)
    queries = qdo[:, 0].reshape(nx * BLK, HD)
    grads = qdo[:, 1].reshape(nx * BLK, HD)
    half = ny * ROWS

    def strided(plane):
        for d in range(1, ny):
            received("y", plane, d)
        rows = pl.ds(plane * half, half)
        keys = kvg[plane, :, 0].reshape(half, HD)
        values = kvg[plane, :, 1].reshape(half, HD)
        s_ref[rows, :] = nt(keys, queries)
        dw_ref[rows, :] = nt(values, grads)

    strided(0)

    def columns(e, d):
        return pl.ds(pl.multiple_of(((g + e) % groups * group + (r + d) % group) * HD, HD), HD)

    w_loads = []
    for e in range(groups):
        to = pl.ds(e * HD, HD)
        load = pltpu.make_async_copy(w_hbm.at[:, columns(e, 0)], wg.at[0, :, to], w_local_sem.at[e])
        load.start()
        w_loads.append(load)
        for d in range(1, group):
            start(("w", d, e), w_hbm.at[:, columns(e, d)], wg.at[group - d, :, to], w_s.at[d, e], w_r.at[d, e], member(d))

    seam_land(0, window_ends)
    seam_received(0, window_ends)
    key_w = win[:, 0].reshape(3 * BLK, HD)
    value_w = win[:, 1].reshape(3 * BLK, HD)
    query_own, grad_own = qdo[0, 0], qdo[0, 1]
    score_w = nt(key_w, query_own) * SCALE
    top_w = jnp.max(score_w, axis=0, keepdims=True)
    p_w = jnp.exp(score_w - top_w)
    sum_w = jnp.sum(p_w, axis=0, keepdims=True)
    dw_w = nt(value_w, grad_own)
    delta_w = jnp.sum(p_w * dw_w, axis=0, keepdims=True)
    o_w = tn(value_w, p_w.astype(BF16))

    seam_over(1, query_ends)
    strided(1)
    chunks = nz * ny
    keys = kvg[:, :, 0].reshape(chunks * ROWS, HD)
    values = kvg[:, :, 1].reshape(chunks * ROWS, HD)
    tops, sums, deltas = [], [], []
    for i in range(nx):
        lanes = pl.ds(i * BLK, BLK)
        spread = jnp.broadcast_to(bias[i][:, None, :], (chunks, ROWS, BLK)).reshape(chunks * ROWS, BLK)
        score = s_ref[:, lanes] * SCALE + spread
        top = jnp.max(score, axis=0, keepdims=True)
        p = jnp.exp(score - top)
        s_ref[:, lanes] = p
        tops.append(top)
        sums.append(jnp.sum(p, axis=0, keepdims=True))
        deltas.append(jnp.sum(p * dw_ref[:, lanes], axis=0, keepdims=True))
    for i in range(nx):
        top, total, delta = tops[i], sums[i], deltas[i]
        if i == 0:
            top = jnp.maximum(tops[0], top_w)
            a, b = jnp.exp(tops[0] - top), jnp.exp(top_w - top)
            total = a * sums[0] + b * sum_w
            delta = a * deltas[0] + b * delta_w
        stats[0, i, 0:1, :] = top
        stats[0, i, 1:2, :] = total
        stats[0, i, 2:3, :] = delta
        stats[0, i, 3:8, :] = jnp.zeros((5, BLK), F32)
    for d in far(nx):
        start(("st", d), stats.at[0], stats.at[nx - d], st_s.at[d], st_r.at[d], at(0, 0, d))
    o_part = tn(values, s_ref[...].astype(BF16))
    for d in far(nx):
        osend[d] = o_part[:, d * BLK:(d + 1) * BLK].astype(BF16)
        start(("o", d), osend.at[d], orecv.at[nx - d], o_s.at[d], o_r.at[d], at(0, 0, d))
    for d in range(1, nx):
        received("st", d)

    logsums, all_deltas = [], []
    for i in range(nx):
        entries = [(stats[p, (i - p) % nx, 0:1, :], stats[p, (i - p) % nx, 1:2, :], stats[p, (i - p) % nx, 2:3, :]) for p in range(nx)]
        top = functools.reduce(jnp.maximum, [e[0] for e in entries])
        logsum = top + jnp.log(sum(e[1] * jnp.exp(e[0] - top) for e in entries))
        logsums.append(logsum)
        all_deltas.append(sum(e[2] * jnp.exp(e[0] - logsum) for e in entries))

    own_rows[0:1, :] = logsums[0]
    own_rows[1:2, :] = all_deltas[0]
    own_rows[2:8, :] = jnp.zeros((6, BLK), F32)
    for way in range(2):
        either(way, lambda copy: copy.start())

    weights, grad_scores = [], []
    for i in range(nx):
        lanes = pl.ds(i * BLK, BLK)
        probability = s_ref[:, lanes] * jnp.exp(tops[i] - logsums[i])
        weights.append(probability.astype(BF16))
        grad_scores.append((probability * (dw_ref[:, lanes] - all_deltas[i]) * SCALE).astype(BF16))
    weights = jnp.concatenate(weights, axis=1)
    grad_scores = jnp.concatenate(grad_scores, axis=1)
    def collect(plane):
        rows = slice(plane * half, (plane + 1) * half)
        gs[plane, :, 0] = nn(grad_scores[rows], queries).astype(BF16).reshape(ny, ROWS, HD)
        gs[plane, :, 1] = nn(weights[rows], grads).astype(BF16).reshape(ny, ROWS, HD)

    collect(1)
    for d in far(ny):
        start(("gy", 1, d), gs.at[1, d], gy.at[1, ny - d], gy_s.at[1, d], gy_r.at[1, d], at(0, d, 0))

    factor_w = jnp.exp(top_w - logsums[0])
    prob_w = p_w * factor_w
    ds_w = (prob_w * (dw_w - all_deltas[0]) * SCALE).astype(BF16)
    own_k = nn(ds_w[BLK:2 * BLK], query_own)
    own_v = nn(prob_w[BLK:2 * BLK].astype(BF16), grad_own)

    attention = o_part[:, :BLK] * jnp.exp(tops[0] - logsums[0]) + o_w * factor_w
    for d in range(1, nx):
        p = nx - d
        received("o", d)
        attention = attention + orecv[p].astype(F32) * jnp.exp(stats[p, (-p) % nx, 0:1, :] - logsums[0])
    attg[0] = attention.astype(BF16)
    for d in range(1, group):
        start(("att", d), attg.at[0], attg.at[group - d], att_s.at[d], att_r.at[d], member(d))

    for way in range(2):
        @pl.when(ways[1 - way][0])
        def _():
            row_copy(way, True).wait_recv()
            row_relay(way).start()

    collect(0)
    for d in far(ny):
        start(("gy", 0, d), gs.at[0, d], gy.at[0, ny - d], gy_s.at[0, d], gy_r.at[0, d], at(0, d, 0))

    seam_land(1, query_ends)

    dq = tn(keys, grad_scores)
    for d in far(nx):
        dqs[d] = dq[:, d * BLK:(d + 1) * BLK].astype(BF16)
        start(("dq", d), dqs.at[d], dqr.at[nx - d], dq_s.at[d], dq_r.at[d], at(0, 0, d))
    dq_own = dq[:, :BLK] + tn(key_w, ds_w)

    for load in w_loads:
        load.wait()
    for d in range(1, group):
        for e in range(groups):
            received("w", d, e)
        received("att", d)
    mixed = tn(attg[...].reshape(group * HD, BLK), wg[...].reshape(group * HD, groups * HD))
    for e in range(1, groups):
        msend[e] = mixed[:, e * HD:(e + 1) * HD].astype(BF16)
        start(("mix", e), msend.at[e], mrecv.at[groups - e], mix_s.at[e], mix_r.at[e], other_group(e))
    mixed_own = mixed[:, :HD]

    total = gs[1, 0].astype(F32)
    for d in range(1, ny):
        received("gy", 1, d)
        total = total + gy[1, ny - d].astype(F32)
    gzs[...] = total.astype(BF16)
    start(("gz", 0), gzs, gzr, gz_s.at[0], gz_r.at[0], at(1, 0, 0))

    for d in range(1, nx):
        received("dq", d)
        dq_own = dq_own + dqr[nx - d].astype(F32)
    out_ref[1] = dq_own.T.astype(BF16)

    seam_received(1, query_ends)
    for way in range(2):
        query_near, grad_near = near[way, 0], near[way, 1]
        score = nt(win[1, 0], query_near) * SCALE
        dw = nt(win[1, 1], grad_near)
        row_copy(way, False).wait_recv()
        probability = jnp.exp(score - near_rows[way, 0:1, :])
        ds = (probability * (dw - near_rows[way, 1:2, :]) * SCALE).astype(BF16)
        own_k = own_k + nn(ds, query_near)
        own_v = own_v + nn(probability.astype(BF16), grad_near)
    out_ref[2, ROWS:, :] = own_k[ROWS:].astype(BF16)
    out_ref[3, ROWS:, :] = own_v[ROWS:].astype(BF16)

    total = gs[0, 0].astype(F32)
    for d in range(1, ny):
        received("gy", 0, d)
        total = total + gy[0, ny - d].astype(F32)

    for e in range(1, groups):
        received("mix", e)
        mixed_own = mixed_own + mrecv[groups - e].astype(F32)
    out_ref[0] = mixed_own.astype(BF16)

    received("gz", 0)
    total = total + gzr[...].astype(F32)
    out_ref[2, :ROWS, :] = (own_k[:ROWS] + total[0]).astype(BF16)
    out_ref[3, :ROWS, :] = (own_v[:ROWS] + total[1]).astype(BF16)

    for copy in started.values():
        copy.wait_send()
    seam_sent(0, window_ends)
    seam_sent(1, query_ends)
    for way in range(2):
        either(way, lambda copy: copy.wait_send())

        @pl.when(ways[1 - way][0])
        def _():
            row_relay(way).wait_send()


def build(mesh, dims, group):
    nz, ny, nx = dims
    heads = mesh.shape["head"]
    groups = heads // group
    chunks = nz * ny

    def shards(queries, key_rows, value_rows, out_weight, strided_index, cotangent):
        width = out_weight.shape[1]
        dma = pltpu.SemaphoreType.DMA
        hbm = pl.BlockSpec(memory_space=pl.ANY)
        vmem = pl.BlockSpec(memory_space=pltpu.VMEM)
        square = lambda n: pltpu.VMEM((n, BLK, HD), BF16)
        pieces = lambda: pltpu.VMEM((nz, ny, 2, ROWS, HD), BF16)
        out = pl.pallas_call(
            functools.partial(kernel, dims, group, heads),
            out_shape=jax.ShapeDtypeStruct((4, BLK, HD), BF16),
            in_specs=[hbm, hbm, hbm, hbm, pl.BlockSpec(memory_space=pltpu.SMEM), hbm],
            out_specs=vmem,
            scratch_shapes=[
                pltpu.VMEM((HD, width), BF16),
                pltpu.VMEM((BLK, width), BF16),
                pltpu.VMEM((3, 2, BLK, HD), BF16),
                pieces(),
                pltpu.VMEM((nx, 2, BLK, HD), BF16),
                pltpu.VMEM((nx, chunks, BLK), F32),
                pltpu.VMEM((group, HD, groups * HD), BF16),
                pltpu.VMEM((nx, nx, 8, BLK), F32),
                square(nx), square(nx),
                square(group),
                square(groups), square(groups),
                square(nx), square(nx),
                pltpu.VMEM((2, 2, BLK, HD), BF16), pltpu.VMEM((8, BLK), F32), pltpu.VMEM((2, 8, BLK), F32), pltpu.VMEM((2, 8, BLK), F32),
                pieces(), pieces(),
                pltpu.VMEM((2, ROWS, HD), BF16), pltpu.VMEM((2, ROWS, HD), BF16),
                pltpu.VMEM((chunks * ROWS, nx * BLK), F32),
                pltpu.VMEM((chunks * ROWS, nx * BLK), F32),
                pltpu.VMEM((2, 2, 2, BLK // 4, HD), BF16), pltpu.VMEM((2, 2, 2, BLK // 4, HD), BF16),
                dma((5,)), dma((groups,)),
                dma((1,)), dma((1,)),
                dma((2, ny)), dma((2, ny)),
                dma((2, 2)), dma((2, 2)),
                dma((2, 2, 4)), dma((2, 2)), dma((2, 2)), dma((2, 2)), dma((2, 2)),
                dma((2,)), dma((2,)), dma((2,)), dma((2,)),
                dma((nx,)), dma((nx,)),
                dma((nx,)), dma((nx,)),
                dma((group, groups)), dma((group, groups)),
                dma((nx,)), dma((nx,)),
                dma((nx,)), dma((nx,)),
                dma((nx,)), dma((nx,)),
                dma((2, ny)), dma((2, ny)),
                dma((1,)), dma((1,)),
                dma((group,)), dma((group,)),
                dma((groups,)), dma((groups,)),
            ],
            compiler_params=pltpu.CompilerParams(
                collective_id=0, has_side_effects=True, vmem_limit_bytes=56 * 2 ** 20
            ),
        )(queries, key_rows, value_rows, out_weight, strided_index, cotangent)
        return tuple(out[i] for i in range(4))

    spread = P("seq", "head")
    return jax.shard_map(
        shards,
        mesh=mesh,
        in_specs=(spread, spread, spread, P("head", None), P("seq", None), P("seq", None)),
        out_specs=(spread,) * 4,
        check_vma=False,
    )


def solution(mesh):
    return build(mesh, GRID, GROUP)
```
